32 devices in a mesh: rows: 8 (over z, y), feat: 4 (over x, core).
Axes of the slice: x: 2, y: 2, z: 4, core: 2. Of those that a mesh axis runs over, the one named last changes fastest.
Arguments:
- features: bfloat16 [16384, 1024], P('rows', 'feat'), may hold values from -6 to 6
- tiles: bfloat16 [5120, 128, 128], P('rows'), may hold values from -0.078125 to 0.078125
- tile_row: int32 [5120], P('rows'), may hold values from 0 to 15, as said below
- tile_panel: int32 [5120], P('rows'), may hold values from 0 to 7
- tile_slot: int32 [5120], P('rows'), may hold values from 0 to 7
- counts: int32 [8], P('rows'), may hold values from 1 to 640, as said below
- need_list: int32 [8, 8, 8], replicated, may hold values from 0 to 15, as said below
- weight: bfloat16 [1024, 1024], replicated, may hold values from -0.1875 to 0.1875
Outputs:
- activations: bfloat16 [16384, 1024], P(('rows', 'feat'))
The draws below stay inside these ranges and needn't reach their ends.
Inputs may be any that keep to these rules, and one draw needn't show every extreme that they name: need_list[g, p] holds 8 distinct tile rows of panel p. Within a row group the slots name distinct (tile_row, tile_panel, tile_slot) triples. `counts`: some row group lists exactly 640 tiles.
All inputs are finite; a program needn't handle non-finite values.
Results may differ from the reference program's by a relative error of at most 0.0049.
Values may be sent and summed in bfloat16 or wider, within the bound.
No kernel may reach another device: no remote copies, remote signals or barrier semaphores. Data moves between devices by JAX's collectives and lax.ppermute only.
A program may use at most 128 MiB of HBM per device.

```python
import jax
import jax.numpy as jnp
from jax import lax

H = 1024
TILE = 128
TPP = 16
MAXT = 640
NEED = 8
VG = 2048
GROUPS = 8
V = 16384


def layout(key):
    keys = jax.random.split(jax.random.fold_in(key, 7), 4)
    need_scores = jax.random.randint(keys[0], (GROUPS, GROUPS, TPP), 0, 65536) * TPP + jnp.arange(TPP, dtype=jnp.int32)
    need_values, need_index = lax.top_k(need_scores, NEED)
    combos = TPP * GROUPS * NEED
    pick_scores = jax.random.randint(keys[1], (GROUPS, combos), 0, 65536) * combos + jnp.arange(combos, dtype=jnp.int32)
    pick_values, picked = lax.top_k(pick_scores, MAXT)
    row_ids = picked // (GROUPS * NEED)
    panel_ids = picked // NEED % GROUPS
    slot_ids = picked % NEED
    base_counts = jax.random.randint(keys[2], (GROUPS,), max(1, MAXT // 8), MAXT // 2 + 1)
    heavy = jax.random.randint(keys[3], (), 0, GROUPS)
    group_counts = jnp.where(jnp.arange(GROUPS, dtype=jnp.int32) == heavy, MAXT, base_counts)
    return (need_index.astype(jnp.int32), row_ids.reshape(-1).astype(jnp.int32), panel_ids.reshape(-1).astype(jnp.int32), slot_ids.reshape(-1).astype(jnp.int32), group_counts.astype(jnp.int32))


def draw_need_list(key, part):
    return layout(key)[0]


def draw_tile_row(key, part):
    return layout(key)[1]


def draw_tile_panel(key, part):
    return layout(key)[2]


def draw_tile_slot(key, part):
    return layout(key)[3]


def draw_counts(key, part):
    return layout(key)[4]


def block_levels(own_key, extent, cuts, smallest, largest):
    loudness = 1.0
    for dim, shards_of in cuts:
        steps = jax.random.uniform(jax.random.fold_in(jax.random.fold_in(own_key, 6), dim), (shards_of,), jnp.float32, smallest / len(cuts), largest / len(cuts))
        loudness = loudness * jnp.repeat(jnp.exp(steps), extent[dim] // shards_of).reshape((-1,) + (1,) * (len(extent) - 1 - dim))
    return loudness


def scatter_about(own_key, shape, spread, limit, cuts=(), kind=jnp.bfloat16):
    values = jax.random.normal(own_key, shape, jnp.float32) * spread
    if len(cuts) > 0:
        values = block_levels(own_key, shape, cuts, -0.22, 0.18) * values
    return jnp.clip(values, min=-limit, max=limit).astype(kind)


def setup_inputs(seed: int = 0) -> dict:
    seeds = jax.random.split(jax.random.key(seed), 9)
    features = scatter_about(seeds[0], (V, H), 1.0, 6.0, ((0, 8), (1, 4)))
    tiles = scatter_about(seeds[1], (GROUPS * MAXT, TILE, TILE), (TILE * MAXT // TPP) ** -0.5, 0.078125, ((0, 8),))
    tile_row = draw_tile_row(jax.random.fold_in(seeds[8], 71), 0)
    tile_panel = draw_tile_panel(jax.random.fold_in(seeds[8], 71), 0)
    tile_slot = draw_tile_slot(jax.random.fold_in(seeds[8], 71), 0)
    counts = draw_counts(jax.random.fold_in(seeds[8], 71), 0)
    need_list = draw_need_list(jax.random.fold_in(seeds[8], 71), 0)
    weight = scatter_about(seeds[7], (H, H), H ** -0.5, 0.1875)
    return {"features": features, "tiles": tiles, "tile_row": tile_row, "tile_panel": tile_panel, "tile_slot": tile_slot, "counts": counts, "need_list": need_list, "weight": weight}


def reference(features, tiles, tile_row, tile_panel, tile_slot, counts, need_list, weight):
    blocks = features.reshape(GROUPS * TPP, TILE, H)

    def group_rows(group):
        first_slot = group * MAXT
        tile_group = lax.dynamic_slice_in_dim(tiles, first_slot, MAXT, 0).astype(jnp.float32)
        row_ids = lax.dynamic_slice_in_dim(tile_row, first_slot, MAXT, 0)
        panel_ids = lax.dynamic_slice_in_dim(tile_panel, first_slot, MAXT, 0)
        slot_ids = lax.dynamic_slice_in_dim(tile_slot, first_slot, MAXT, 0)
        table = need_list[group]
        block_ids = (panel_ids * TPP + table[panel_ids, slot_ids]).astype(jnp.int32)
        fetched = blocks[block_ids].astype(jnp.float32)
        product = jnp.einsum("sij,sjh->sih", tile_group, fetched, precision=lax.Precision.HIGHEST)
        live_slot = (jnp.arange(MAXT, dtype=jnp.int32) < counts[group]).astype(product.dtype)
        product = product * live_slot[:, None, None]
        return jax.ops.segment_sum(product, row_ids, num_segments=TPP)

    summed = lax.map(group_rows, jnp.arange(GROUPS, dtype=jnp.int32))
    rounded = summed.reshape(GROUPS * VG, H).astype(jnp.bfloat16)
    mixed = jnp.dot(rounded, weight, preferred_element_type=jnp.float32)
    return jnp.maximum(mixed, 0.0).astype(jnp.bfloat16)
```

```python
import functools

import jax
import jax.numpy as jnp
from jax import lax
from jax.experimental import pallas as pl
from jax.experimental.pallas import tpu as pltpu
from jax.sharding import PartitionSpec as P

TILE = 128
TPP = 16
NEED = 8
PER_PANEL = TPP * NEED
VMEM_LIMIT = 60 * 1024 * 1024


def aggregate_kernel(entries, meta, table, tiles, source, out, dense, feats, count, tile_sem, feat_sem):
    def fetch(entry):
        buf = lax.rem(entry, 2)
        base = meta[entry] * PER_PANEL

        def row_step(row, total):
            for k in range(NEED):
                slot = table[base + row * NEED + k]
                rows = pl.ds(pl.multiple_of(row * TILE, TILE), TILE)
                cols = pl.ds(k * TILE, TILE)

                @pl.when(slot > 0)
                def _():
                    pltpu.make_async_copy(tiles.at[slot - 1], dense.at[buf, rows, cols], tile_sem.at[buf]).start()

                @pl.when(slot == 0)
                def _():
                    dense[buf, rows, cols] = jnp.zeros((TILE, TILE), jnp.bfloat16)

                total = total + jnp.where(slot > 0, 1, 0)
            return total

        count[buf] = lax.fori_loop(0, TPP, row_step, 0)

    copy = pltpu.make_async_copy(source, feats, feat_sem)
    copy.start()
    fetch(0)
    out[...] = jnp.zeros_like(out)
    copy.wait()

    def step(entry, carry):
        buf = lax.rem(entry, 2)

        @pl.when(entry + 1 < entries)
        def _():
            fetch(entry + 1)

        def wait_one(i, c):
            pltpu.make_async_copy(tiles.at[0], dense.at[buf, pl.ds(0, TILE), pl.ds(0, TILE)], tile_sem.at[buf]).wait()
            return c

        lax.fori_loop(0, count[buf], wait_one, 0)
        block = 512

        def part(m, c):
            rows = pl.ds(pl.multiple_of(m * block, block), block)
            out[rows, :] += jnp.dot(dense[buf, rows, :], feats[entry], preferred_element_type=jnp.float32)
            return c

        lax.fori_loop(0, TPP * TILE // block, part, 0)
        return carry

    lax.fori_loop(0, entries, step, 0)


def aggregate(meta, table, tiles, source):
    entries, depth, width = source.shape
    return pl.pallas_call(
        functools.partial(aggregate_kernel, entries),
        out_shape=jax.ShapeDtypeStruct((TPP * TILE, width), jnp.float32),
        in_specs=[
            pl.BlockSpec(memory_space=pltpu.SMEM),
            pl.BlockSpec(memory_space=pltpu.SMEM),
            pl.BlockSpec(memory_space=pl.ANY),
            pl.BlockSpec(memory_space=pl.ANY),
        ],
        out_specs=pl.BlockSpec(memory_space=pltpu.VMEM),
        scratch_shapes=[
            pltpu.VMEM((2, TPP * TILE, depth), jnp.bfloat16),
            pltpu.VMEM((entries, depth, width), jnp.bfloat16),
            pltpu.SMEM((2,), jnp.int32),
            pltpu.SemaphoreType.DMA((2,)),
            pltpu.SemaphoreType.DMA,
        ],
        compiler_params=pltpu.CompilerParams(vmem_limit_bytes=VMEM_LIMIT),
        name="aggregate",
    )(meta, table, tiles, source)


def product_kernel(x, w, out):
    blocks, rows, width = x.shape
    total = jnp.dot(x[0], w[0:width, :], preferred_element_type=jnp.float32)
    for f in range(1, blocks):
        total += jnp.dot(x[f], w[f * width : (f + 1) * width, :], preferred_element_type=jnp.float32)
    out[...] = jnp.maximum(total, 0.0).astype(out.dtype)


def product(x, w):
    blocks, rows, width = x.shape
    depth, cols = w.shape
    step = 256
    return pl.pallas_call(
        product_kernel,
        grid=(cols // step,),
        out_shape=jax.ShapeDtypeStruct((rows, cols), jnp.bfloat16),
        in_specs=[
            pl.BlockSpec((blocks, rows, width), lambda j: (0, 0, 0)),
            pl.BlockSpec((depth, step), lambda j: (0, j)),
        ],
        out_specs=pl.BlockSpec((rows, step), lambda j: (0, j)),
        compiler_params=pltpu.CompilerParams(vmem_limit_bytes=32 * 1024 * 1024),
        name="product",
    )(x, w)


def slot_table(groups, tile_row, tile_panel, tile_slot, counts):
    slots = lax.iota(jnp.int32, tile_row.shape[0])
    key = (tile_panel * TPP + tile_row) * NEED + tile_slot
    key = jnp.where(slots < counts[0], key, -1)
    places = lax.iota(jnp.int32, groups * PER_PANEL)
    return jnp.max(jnp.where(key[None, :] == places[:, None], slots[None, :] + 1, 0), axis=1)


def per_device(features, tiles, tile_row, tile_panel, tile_slot, counts, need_list, weight):
    shard_width = features.shape[1]
    groups = lax.axis_size("rows")
    feat = lax.axis_size("feat")
    own_group = lax.axis_index("rows")
    wanted = lax.dynamic_index_in_dim(need_list, own_group, 1, keepdims=False)
    outgoing = features.reshape(TPP, TILE, shard_width).at[wanted.reshape(-1)].get(mode="promise_in_bounds")
    outgoing = outgoing.reshape(groups, NEED * TILE, shard_width)
    arrived = lax.all_to_all(outgoing, "rows", split_axis=0, concat_axis=0, tiled=True)
    table = slot_table(groups, tile_row, tile_panel, tile_slot, counts)
    summed = aggregate(lax.iota(jnp.int32, groups), table, tiles, arrived)
    rounded = summed.astype(jnp.bfloat16).reshape(feat, -1, shard_width)
    rows_full = lax.all_to_all(rounded, "feat", split_axis=0, concat_axis=0, tiled=True)
    return product(rows_full, weight)


def solution(mesh):
    return jax.shard_map(
        per_device,
        mesh=mesh,
        in_specs=(
            P("rows", "feat"),
            P("rows", None, None),
            P("rows"),
            P("rows"),
            P("rows"),
            P("rows"),
            P(),
            P(),
        ),
        out_specs=P(("rows", "feat"), None),
        check_vma=False,
    )
```

```python
import functools

import jax
import jax.numpy as jnp
from jax import lax
from jax.experimental import pallas as pl
from jax.experimental.pallas import tpu as pltpu
from jax.sharding import PartitionSpec as P

TILE = 128
TPP = 16
NEED = 8
PER_PANEL = TPP * NEED
ROWS = TPP * TILE
DEPTH = NEED * TILE
VMEM_LIMIT = 44 * 1024 * 1024


def aggregate_kernel(plan, n_sources, first, blocks, panels, table, need, tiles, *refs):
    sources = refs[:n_sources]
    refs = refs[n_sources:]
    start_total = None if first else refs[0]
    refs = refs if first else refs[1:]
    if blocks:
        outs, total, (dense, feats, count, tile_sem) = refs[:blocks], refs[blocks], refs[blocks + 1 :]
    else:
        total, dense, feats, count, tile_sem = refs
    entries = len(plan)

    def fetch(entry):
        buf = lax.rem(entry, 2)
        base = panels[entry] * PER_PANEL

        def row_step(row, live):
            for k in range(NEED):
                slot = table[base + row * NEED + k]
                rows = pl.ds(pl.multiple_of(row * TILE, TILE), TILE)
                cols = pl.ds(k * TILE, TILE)

                @pl.when(slot > 0)
                def _():
                    pltpu.make_async_copy(tiles.at[slot - 1], dense.at[buf, rows, cols], tile_sem.at[buf]).start()

                @pl.when(slot == 0)
                def _():
                    dense[buf, rows, cols] = jnp.zeros((TILE, TILE), jnp.bfloat16)

                live = live + jnp.where(slot > 0, 1, 0)
            return live

        count[buf] = lax.fori_loop(0, TPP, row_step, 0)

    fetch(0)
    for e, pieces in enumerate(plan):
        for source, column, width, whole in pieces:
            cols = pl.ds(column, width)
            if whole:
                for k in range(NEED):
                    row = pl.multiple_of(need[panels[e] * NEED + k] * TILE, TILE)
                    feats[e, pl.ds(k * TILE, TILE), cols] = sources[source][pl.ds(row, TILE), :]
            else:
                feats[e, :, cols] = sources[source][...]
    if first:
        total[...] = jnp.zeros_like(total)
    else:
        total[...] = start_total[...]

    def step(entry, carry):
        buf = lax.rem(entry, 2)

        @pl.when(entry + 1 < entries)
        def _():
            fetch(entry + 1)

        def wait_one(i, c):
            pltpu.make_async_copy(tiles.at[0], dense.at[buf, pl.ds(0, TILE), pl.ds(0, TILE)], tile_sem.at[buf]).wait()
            return c

        lax.fori_loop(0, count[buf], wait_one, 0)
        total[...] += jnp.dot(dense[buf], feats[entry], preferred_element_type=jnp.float32)
        return carry

    lax.fori_loop(0, entries, step, 0)
    if blocks:
        own = lax.axis_index("feat")
        size = ROWS // blocks
        for m in range(blocks):
            rows = pl.ds(pl.multiple_of((own ^ m) * size, size), size)
            outs[m][...] = total[rows, :].astype(jnp.bfloat16)


def aggregate(plan, panels, table, need, tiles, sources, start_total, width, blocks=0):
    entries = len(plan)
    first = start_total is None
    smem = pl.BlockSpec(memory_space=pltpu.SMEM)
    vmem = pl.BlockSpec(memory_space=pltpu.VMEM)
    hbm = pl.BlockSpec(memory_space=pl.ANY)
    scratch = [
        pltpu.VMEM((2, ROWS, DEPTH), jnp.bfloat16),
        pltpu.VMEM((entries, DEPTH, width), jnp.bfloat16),
        pltpu.SMEM((2,), jnp.int32),
        pltpu.SemaphoreType.DMA((2,)),
    ]
    if blocks:
        out_shape = [jax.ShapeDtypeStruct((ROWS // blocks, width), jnp.bfloat16)] * blocks
        out_specs = [vmem] * blocks
        scratch = [pltpu.VMEM((ROWS, width), jnp.float32)] + scratch
    else:
        out_shape = jax.ShapeDtypeStruct((ROWS, width), jnp.float32)
        out_specs = vmem
    return pl.pallas_call(
        functools.partial(aggregate_kernel, plan, len(sources), first, blocks),
        out_shape=out_shape,
        in_specs=[smem, smem, smem, hbm] + [vmem] * len(sources) + ([] if first else [vmem]),
        out_specs=out_specs,
        scratch_shapes=scratch,
        compiler_params=pltpu.CompilerParams(vmem_limit_bytes=VMEM_LIMIT),
        cost_estimate=pl.CostEstimate(
            flops=2 * entries * ROWS * DEPTH * width,
            bytes_accessed=entries * PER_PANEL * TILE * TILE * 2,
            transcendentals=0,
        ),
        name="aggregate",
    )(panels, table, need, tiles, *sources, *(() if first else (start_total,)))


def product_kernel(blocks, *refs):
    w, out = refs[blocks], refs[blocks + 1]
    width = refs[0].shape[1]
    own = lax.axis_index("feat")
    total = None
    for m in range(blocks):
        rows = pl.ds(pl.multiple_of((own ^ m) * width, width), width)
        term = jnp.dot(refs[m][...], w[rows, :], preferred_element_type=jnp.float32)
        total = term if total is None else total + term
    out[...] = jnp.maximum(total, 0.0).astype(out.dtype)


def product(parts, w):
    blocks = len(parts)
    rows, width = parts[0].shape
    depth, cols = w.shape
    step = 256
    return pl.pallas_call(
        functools.partial(product_kernel, blocks),
        grid=(cols // step,),
        out_shape=jax.ShapeDtypeStruct((rows, cols), jnp.bfloat16),
        in_specs=[pl.BlockSpec((rows, width), lambda j: (0, 0))] * blocks
        + [pl.BlockSpec((depth, step), lambda j: (0, j))],
        out_specs=pl.BlockSpec((rows, step), lambda j: (0, j)),
        compiler_params=pltpu.CompilerParams(vmem_limit_bytes=32 * 1024 * 1024),
        name="product",
    )(*parts, w)


def slot_table(groups, tile_row, tile_panel, tile_slot, counts):
    slots = lax.iota(jnp.int32, tile_row.shape[0])
    key = (tile_panel * TPP + tile_row) * NEED + tile_slot
    key = jnp.where(slots < counts[0], key, -1)
    places = lax.iota(jnp.int32, groups * PER_PANEL)
    return jnp.max(jnp.where(key[None, :] == places[:, None], slots[None, :] + 1, 0), axis=1)


def ring_group(place, groups):
    place = lax.rem(place + 2 * groups, groups)
    return jnp.where(place < groups // 2, 2 * place, 2 * (groups - 1 - place) + 1)


def ring_pairs(groups, way):
    order = [2 * p if p < groups // 2 else 2 * (groups - 1 - p) + 1 for p in range(groups)]
    return [(order[p], order[(p + way) % groups]) for p in range(groups)]


def per_device(features, tiles, tile_row, tile_panel, tile_slot, counts, need_list, weight):
    width = features.shape[1]
    half = width // 2
    groups = lax.axis_size("rows")
    blocks = lax.axis_size("feat")
    far = groups // 2
    own = lax.axis_index("rows")
    place = jnp.where(own % 2 == 0, own // 2, groups - 1 - own // 2)

    def group_at(offset):
        return ring_group(place + offset, groups)

    def needed(array, reader, panel):
        ids = need_list[reader, panel]
        return array.reshape(TPP, TILE, -1).at[ids].get(mode="promise_in_bounds").reshape(DEPTH, -1)

    def send(array, way):
        return lax.ppermute(array, "rows", ring_pairs(groups, way))

    table = slot_table(groups, tile_row, tile_panel, tile_slot, counts)
    need = need_list[own].reshape(-1)

    def panels(*offsets):
        return jnp.stack([group_at(o) for o in offsets]).astype(jnp.int32)

    def add(total, offsets, pieces, final=0):
        plan, sources = [], []
        for entry in pieces:
            column, steps = 0, []
            for array, whole in entry:
                steps.append((len(sources), column, array.shape[1], whole))
                sources.append(array)
                column += array.shape[1]
            plan.append(tuple(steps))
        return aggregate(tuple(plan), panels(*offsets), table, need, tiles, sources, total, width, final)

    cuts = 2 if width % (2 * TILE) == 0 else 1
    part = width // cuts
    long_way = [1, -1][:cuts]
    held = {way: [(features[:, c * part : (c + 1) * part], True) for c in range(cuts)] for way in (1, -1)}
    total = add(None, [0], [[(features, True)]])
    for d in range(1, far + 1):
        fresh = {}
        for c in range(cuts):
            for way in (1, -1):
                last = far if way == long_way[c] else far - 1
                if d > last:
                    continue
                array = held[way][c][0]
                if c == 0 and d > 1:
                    total, array = lax.optimization_barrier((total, array))
                if d == last:
                    array = needed(array, group_at(way), group_at(way - way * d))
                fresh[way, c] = (send(array, way), d < last)
        if d == far:
            break
        for way in (1, -1):
            held[way] = [fresh[way, c] for c in range(cuts)]
        if d > 1:
            total = add(total, [1 - d, d - 1], [before[1], before[-1]])
        before = dict(held)
    total = add(total, [1 - far, far - 1], [before[1], before[-1]])
    parts = add(total, [far], [[fresh[long_way[c], c] for c in range(cuts)]], blocks)
    arrived = [parts[0]]
    for m in range(1, blocks):
        arrived.append(lax.ppermute(parts[m], "feat", [(f, f ^ m) for f in range(blocks)]))
    return product(arrived, weight)


def solution(mesh):
    return jax.shard_map(
        per_device,
        mesh=mesh,
        in_specs=(
            P("rows", "feat"),
            P("rows", None, None),
            P("rows"),
            P("rows"),
            P("rows"),
            P("rows"),
            P(),
            P(),
        ),
        out_specs=P(("rows", "feat"), None),
        check_vma=False,
    )
```

```python
import functools

import jax
import jax.numpy as jnp
from jax import lax
from jax.experimental import pallas as pl
from jax.experimental.pallas import tpu as pltpu
from jax.sharding import PartitionSpec as P


TILE = 128
TPP = 16
NEED = 8
PER_PANEL = TPP * NEED
ROWS = TPP * TILE
DEPTH = NEED * TILE
VMEM_LIMIT = 34 * 1024 * 1024
PIECES = 2


def densify_kernel(offsets, groups, table, tiles, out, dense, live, tile_sem, out_sem):
    buffers = dense.shape[0]
    entries = out.shape[0]

    def fetch(entry):
        buf = entry % buffers
        base = group_at(offsets[entry], groups) * PER_PANEL

        def row_step(row, found):
            for k in range(NEED):
                slot = table[base + row * NEED + k]
                rows = pl.ds(pl.multiple_of(row * TILE, TILE), TILE)
                cols = pl.ds(k * TILE, TILE)

                @pl.when(slot > 0)
                def _():
                    pltpu.make_async_copy(tiles.at[slot - 1], dense.at[buf, rows, cols], tile_sem.at[buf]).start()

                @pl.when(slot == 0)
                def _():
                    dense[buf, rows, cols] = jnp.zeros((TILE, TILE), jnp.bfloat16)

                found = found + jnp.where(slot > 0, 1, 0)
            return found

        live[buf] = lax.fori_loop(0, TPP, row_step, 0)

    def store(entry):
        buf = entry % buffers
        return pltpu.make_async_copy(dense.at[buf], out.at[entry], out_sem.at[buf])

    def arrive(entry):
        buf = entry % buffers

        def wait_one(i, c):
            pltpu.make_async_copy(tiles.at[0], dense.at[buf, pl.ds(0, TILE), pl.ds(0, TILE)], tile_sem.at[buf]).wait()
            return c

        lax.fori_loop(0, live[buf], wait_one, 0)
        store(entry).start()

    for entry in range(entries):
        if entry >= buffers:
            store(entry - buffers).wait()
        fetch(entry)
        if entry:
            arrive(entry - 1)
    arrive(entries - 1)
    for entry in range(max(0, entries - buffers), entries):
        store(entry).wait()


def densify(offsets, groups, table, tiles):
    smem = pl.BlockSpec(memory_space=pltpu.SMEM)
    hbm = pl.BlockSpec(memory_space=pl.ANY)
    buffers = 4
    entries = len(offsets)
    return pl.pallas_call(
        functools.partial(densify_kernel, offsets, groups),
        out_shape=jax.ShapeDtypeStruct((entries, ROWS, DEPTH), jnp.bfloat16),
        in_specs=[smem, hbm],
        out_specs=hbm,
        scratch_shapes=[
            pltpu.VMEM((buffers, ROWS, DEPTH), jnp.bfloat16),
            pltpu.SMEM((buffers,), jnp.int32),
            pltpu.SemaphoreType.DMA((buffers,)),
            pltpu.SemaphoreType.DMA((buffers,)),
        ],
        compiler_params=pltpu.CompilerParams(vmem_limit_bytes=44 * 1024 * 1024),
        cost_estimate=pl.CostEstimate(flops=0, bytes_accessed=4 * entries * ROWS * DEPTH, transcendentals=0),
        name="densify",
    )(table, tiles)


def aggregate_kernel(base, plan, offsets, groups, n_sources, first, blocks, need, dense_hbm, *refs):
    sources = refs[:n_sources]
    refs = refs[n_sources:]
    start_total = None if first else refs[0]
    refs = refs if first else refs[1:]
    if blocks:
        outs, total, (dense, feats, sem) = refs[:blocks], refs[blocks], refs[blocks + 1 :]
    else:
        total, dense, feats, sem = refs
    entries = len(plan)
    size = ROWS // PIECES

    def load(e, p):
        rows = pl.ds(p * size, size)
        return pltpu.make_async_copy(dense_hbm.at[base + e, rows, :], dense.at[e, rows, :], sem.at[e, p])

    for e in range(entries):
        for p in range(PIECES):
            load(e, p).start()
    for e, pieces in enumerate(plan):
        for source, column, width, whole in pieces:
            cols = pl.ds(column, width)
            if whole:
                for k in range(NEED):
                    rows = needed_rows(need, groups, 0, offsets[e], k)
                    feats[e, pl.ds(k * TILE, TILE), cols] = sources[source][rows, :]
            else:
                feats[e, :, cols] = sources[source][...]
    for e in range(entries):
        for p in range(PIECES):
            rows = pl.ds(p * size, size)
            load(e, p).wait()
            term = jnp.dot(dense[e, rows, :], feats[e], preferred_element_type=jnp.float32)
            if e:
                total[rows, :] += term
            elif first:
                total[rows, :] = term
            else:
                total[rows, :] = start_total[rows, :] + term
    if blocks:
        own = lax.axis_index("feat")
        size = ROWS // blocks
        for m in range(blocks):
            rows = pl.ds(pl.multiple_of((own ^ m) * size, size), size)
            outs[m][...] = total[rows, :].astype(jnp.bfloat16)


def aggregate(base, plan, offsets, groups, need, dense, sources, start_total, width, blocks=0):
    entries = len(plan)
    first = start_total is None
    smem = pl.BlockSpec(memory_space=pltpu.SMEM)
    vmem = pl.BlockSpec(memory_space=pltpu.VMEM)
    hbm = pl.BlockSpec(memory_space=pl.ANY)
    scratch = [
        pltpu.VMEM((entries, ROWS, DEPTH), jnp.bfloat16),
        pltpu.VMEM((entries, DEPTH, width), jnp.bfloat16),
        pltpu.SemaphoreType.DMA((entries, PIECES)),
    ]
    if blocks:
        out_shape = [jax.ShapeDtypeStruct((ROWS // blocks, width), jnp.bfloat16)] * blocks
        out_specs = [vmem] * blocks
        scratch = [pltpu.VMEM((ROWS, width), jnp.float32)] + scratch
    else:
        out_shape = jax.ShapeDtypeStruct((ROWS, width), jnp.float32)
        out_specs = vmem
    return pl.pallas_call(
        functools.partial(aggregate_kernel, base, plan, offsets, groups, len(sources), first, blocks),
        out_shape=out_shape,
        in_specs=[smem, hbm] + [vmem] * len(sources) + ([] if first else [vmem]),
        out_specs=out_specs,
        scratch_shapes=scratch,
        compiler_params=pltpu.CompilerParams(vmem_limit_bytes=VMEM_LIMIT),
        cost_estimate=pl.CostEstimate(
            flops=2 * entries * ROWS * DEPTH * width,
            bytes_accessed=entries * PER_PANEL * TILE * TILE * 2,
            transcendentals=0,
        ),
        name="aggregate",
    )(need, dense, *sources, *(() if first else (start_total,)))


def product_kernel(blocks, *refs):
    w, out = refs[blocks], refs[blocks + 1]
    width = refs[0].shape[1]
    own = lax.axis_index("feat")
    total = None
    for m in range(blocks):
        rows = pl.ds(pl.multiple_of((own ^ m) * width, width), width)
        term = jnp.dot(refs[m][...], w[rows, :], preferred_element_type=jnp.float32)
        total = term if total is None else total + term
    out[...] = jnp.maximum(total, 0.0).astype(out.dtype)


def product(parts, w):
    blocks = len(parts)
    rows, width = parts[0].shape
    depth, cols = w.shape
    step = 256
    return pl.pallas_call(
        functools.partial(product_kernel, blocks),
        grid=(cols // step,),
        out_shape=jax.ShapeDtypeStruct((rows, cols), jnp.bfloat16),
        in_specs=[pl.BlockSpec((rows, width), lambda j: (0, 0))] * blocks
        + [pl.BlockSpec((depth, step), lambda j: (0, j))],
        out_specs=pl.BlockSpec((rows, step), lambda j: (0, j)),
        compiler_params=pltpu.CompilerParams(vmem_limit_bytes=32 * 1024 * 1024),
        name="product",
    )(*parts, w)


def slot_table(groups, tile_row, tile_panel, tile_slot, counts):
    slots = lax.iota(jnp.int32, tile_row.shape[0])
    key = (tile_panel * TPP + tile_row) * NEED + tile_slot
    key = jnp.where(slots < counts[0], key, -1)
    places = lax.iota(jnp.int32, groups * PER_PANEL)
    return jnp.max(jnp.where(key[None, :] == places[:, None], slots[None, :] + 1, 0), axis=1)


def group_at(offset, groups):
    own = lax.axis_index("rows")
    place = jnp.where(lax.rem(own, 2) == 0, lax.div(own, 2), groups - 1 - lax.div(own, 2))
    place = lax.rem(place + offset + groups, groups)
    return jnp.where(place < groups // 2, 2 * place, 2 * (groups - 1 - place) + 1)


def needed_rows(need, groups, reader, offset, k):
    tile = need[(group_at(reader, groups) * groups + group_at(offset, groups)) * NEED + k]
    return pl.ds(pl.multiple_of(tile * TILE, TILE), TILE)


def pick_kernel(reader, offset, groups, need, source, out):
    for k in range(NEED):
        out[pl.ds(k * TILE, TILE), :] = source[needed_rows(need, groups, reader, offset, k), :]


def pick(need, source, reader, offset, groups):
    vmem = pl.BlockSpec(memory_space=pltpu.VMEM)
    return pl.pallas_call(
        functools.partial(pick_kernel, reader, offset, groups),
        out_shape=jax.ShapeDtypeStruct((DEPTH, source.shape[1]), source.dtype),
        in_specs=[pl.BlockSpec(memory_space=pltpu.SMEM), vmem],
        out_specs=vmem,
        compiler_params=pltpu.CompilerParams(vmem_limit_bytes=4 * 1024 * 1024),
        name="pick",
    )(need, source)


def ring_pairs(groups, way):
    order = [2 * p if p < groups // 2 else 2 * (groups - 1 - p) + 1 for p in range(groups)]
    return [(order[p], order[(p + way) % groups]) for p in range(groups)]


def per_device(features, tiles, tile_row, tile_panel, tile_slot, counts, need_list, weight):
    width = features.shape[1]
    groups = lax.axis_size("rows")
    blocks = lax.axis_size("feat")
    far = groups // 2

    def send(array, way):
        return lax.ppermute(array, "rows", ring_pairs(groups, way))

    table = slot_table(groups, tile_row, tile_panel, tile_slot, counts)
    need = need_list.reshape(-1)

    stages = [[0]] + [[-d, d] for d in range(1, far)] + [[far]]
    dense = densify([o for stage in stages for o in stage], groups, table, tiles)

    def add(total, d, pieces, final=0):
        plan, sources = [], []
        for entry in pieces:
            column, steps = 0, []
            for array, whole in entry:
                steps.append((len(sources), column, array.shape[1], whole))
                sources.append(array)
                column += array.shape[1]
            plan.append(tuple(steps))
        base = sum(len(stage) for stage in stages[:d])
        return aggregate(base, tuple(plan), stages[d], groups, need, dense, sources, total, width, final)

    cuts = 2 if width % (2 * TILE) == 0 else 1
    part = width // cuts
    long_way = [1, -1][:cuts]
    held = {way: [(features[:, c * part : (c + 1) * part], True) for c in range(cuts)] for way in (1, -1)}
    total = add(None, 0, [[(features, True)]])
    for d in range(1, far + 1):
        fresh = {}
        for c in range(cuts):
            for way in (1, -1):
                last = far if way == long_way[c] else far - 1
                if d > last:
                    continue
                array = held[way][c][0]
                if d == last:
                    array = pick(need, array, way, way - way * d, groups)
                fresh[way, c] = (send(array, way), d < last)
        if d == far:
            break
        for way in (1, -1):
            held[way] = [fresh[way, c] for c in range(cuts)]
        if d > 1:
            total = add(total, d - 1, [before[1], before[-1]])
        before = dict(held)
    total = add(total, far - 1, [before[1], before[-1]])
    parts = add(total, far, [[fresh[long_way[c], c] for c in range(cuts)]], blocks)
    arrived = [parts[0]]
    for m in range(1, blocks):
        arrived.append(lax.ppermute(parts[m], "feat", [(f, f ^ m) for f in range(blocks)]))
    return product(arrived, weight)


def solution(mesh):
    return jax.shard_map(
        per_device,
        mesh=mesh,
        in_specs=(
            P("rows", "feat"),
            P("rows", None, None),
            P("rows"),
            P("rows"),
            P("rows"),
            P("rows"),
            P(),
            P(),
        ),
        out_specs=P(("rows", "feat"), None),
        check_vma=False,
    )
```

```python
import functools

import jax
import jax.numpy as jnp
from jax import lax
from jax.experimental import pallas as pl
from jax.experimental.pallas import tpu as pltpu
from jax.sharding import PartitionSpec as P


TILE = 128
TPP = 16
NEED = 8
PER_PANEL = TPP * NEED
ROWS = TPP * TILE
DEPTH = NEED * TILE
MIB = 1024 * 1024
RESIDENT_PANELS = 8
RESIDENT_LIMIT = 9 * MIB
STREAM_LIMIT = 14 * MIB
DENSIFY_LIMIT = 38 * MIB
PIECES = 2


def place_tiles(panel, table, tiles, dense, sem):
    base = panel * PER_PANEL

    def row_step(row, found):
        for k in range(NEED):
            slot = table[base + row * NEED + k]
            rows = pl.ds(pl.multiple_of(row * TILE, TILE), TILE)
            cols = pl.ds(k * TILE, TILE)

            @pl.when(slot > 0)
            def _():
                pltpu.make_async_copy(tiles.at[slot - 1], dense.at[rows, cols], sem).start()

            @pl.when(slot == 0)
            def _():
                dense[rows, cols] = jnp.zeros((TILE, TILE), jnp.bfloat16)

            found = found + jnp.where(slot > 0, 1, 0)
        return found

    return lax.fori_loop(0, TPP, row_step, 0)


def await_tiles(found, tiles, dense, sem):
    def wait_one(i, c):
        pltpu.make_async_copy(tiles.at[0], dense.at[pl.ds(0, TILE), pl.ds(0, TILE)], sem).wait()
        return c

    lax.fori_loop(0, found, wait_one, 0)


def densify_kernel(stages, resident, groups, table, tiles, *refs):
    outs, (dense, tile_sem, out_sem) = refs[: len(stages)], refs[len(stages) :]
    entries = [(out, e, o) for out, stage in zip(outs, stages) for e, o in enumerate(stage)]
    if resident:
        found = [
            place_tiles(group_at(o, groups), table, tiles, out.at[e], tile_sem.at[0]) for out, e, o in entries
        ]
        out, e, o = entries[0]
        await_tiles(sum(found), tiles, out.at[e], tile_sem.at[0])
        return
    buffers = dense.shape[0]

    def store(i):
        out, e, _ = entries[i]
        return pltpu.make_async_copy(dense.at[i % buffers], out.at[e], out_sem.at[i % buffers])

    for i, (out, e, o) in enumerate(entries):
        buf = i % buffers
        if i >= buffers:
            store(i - buffers).wait()
        found = place_tiles(group_at(o, groups), table, tiles, dense.at[buf], tile_sem.at[buf])
        await_tiles(found, tiles, dense.at[buf], tile_sem.at[buf])
        store(i).start()
    for i in range(max(0, len(entries) - buffers), len(entries)):
        store(i).wait()


def densify(stages, resident, groups, table, tiles):
    buffers = 1 if resident else 2
    out_space = pltpu.VMEM if resident else pl.ANY
    entries = sum(len(stage) for stage in stages)
    return pl.pallas_call(
        functools.partial(densify_kernel, stages, resident, groups),
        out_shape=[jax.ShapeDtypeStruct((len(stage), ROWS, DEPTH), jnp.bfloat16) for stage in stages],
        in_specs=[pl.BlockSpec(memory_space=pltpu.SMEM), pl.BlockSpec(memory_space=pl.ANY)],
        out_specs=[pl.BlockSpec(memory_space=out_space)] * len(stages),
        scratch_shapes=[
            pltpu.VMEM((8, TILE) if resident else (buffers, ROWS, DEPTH), jnp.bfloat16),
            pltpu.SemaphoreType.DMA((buffers,)),
            pltpu.SemaphoreType.DMA((buffers,)),
        ],
        compiler_params=pltpu.CompilerParams(vmem_limit_bytes=max(10 * MIB, DENSIFY_LIMIT - 2 * entries * ROWS * DEPTH)),
        cost_estimate=pl.CostEstimate(flops=0, bytes_accessed=2 * entries * ROWS * DEPTH, transcendentals=0),
        name="densify",
    )(table, tiles)


def aggregate_kernel(plan, offsets, groups, n_sources, first, resident, blocks, need, dense, *refs):
    sources = refs[:n_sources]
    refs = refs[n_sources:]
    start_total = None if first else refs[0]
    refs = refs if first else refs[1:]
    if blocks:
        outs, total, (streamed, feats, sem) = refs[:blocks], refs[blocks], refs[blocks + 1 :]
    else:
        total, streamed, feats, sem = refs
    entries = len(plan)
    size = ROWS // PIECES

    def load(e, p):
        rows = pl.ds(pl.multiple_of(p * size, size), size)
        return pltpu.make_async_copy(dense.at[e, rows, :], streamed.at[e, rows, :], sem.at[e, p])

    if not resident:
        for e in range(entries):
            for p in range(PIECES):
                load(e, p).start()
    for e, pieces in enumerate(plan):
        for source, column, width, whole in pieces:
            cols = pl.ds(column, width)
            if whole:
                for k in range(NEED):
                    rows = needed_rows(need, groups, 0, offsets[e], k)
                    feats[e, pl.ds(k * TILE, TILE), cols] = sources[source][rows, :]
            else:
                feats[e, :, cols] = sources[source][...]
    if resident:
        for e in range(entries):
            term = jnp.dot(dense[e], feats[e], preferred_element_type=jnp.float32)
            if e:
                total[...] += term
            else:
                total[...] = term if first else start_total[...] + term
    else:
        total[...] = jnp.zeros_like(total) if first else start_total[...]
        for e in range(entries):

            def part(p, c):
                rows = pl.ds(pl.multiple_of(p * size, size), size)
                load(e, p).wait()
                total[rows, :] += jnp.dot(streamed[e, rows, :], feats[e], preferred_element_type=jnp.float32)
                return c

            lax.fori_loop(0, PIECES, part, 0)
    if blocks:
        own = lax.axis_index("feat")
        size = ROWS // blocks
        for m in range(blocks):
            rows = pl.ds(pl.multiple_of((own ^ m) * size, size), size)
            outs[m][...] = total[rows, :].astype(jnp.bfloat16)


def aggregate(plan, offsets, groups, need, dense, resident, sources, start_total, width, blocks=0):
    entries = len(plan)
    first = start_total is None
    smem = pl.BlockSpec(memory_space=pltpu.SMEM)
    vmem = pl.BlockSpec(memory_space=pltpu.VMEM)
    hbm = pl.BlockSpec(memory_space=pl.ANY)
    scratch = [
        pltpu.VMEM((8, TILE) if resident else (entries, ROWS, DEPTH), jnp.bfloat16),
        pltpu.VMEM((entries, DEPTH, width), jnp.bfloat16),
        pltpu.SemaphoreType.DMA((entries, PIECES)),
    ]
    if blocks:
        out_shape = [jax.ShapeDtypeStruct((ROWS // blocks, width), jnp.bfloat16)] * blocks
        out_specs = [vmem] * blocks
        scratch = [pltpu.VMEM((ROWS, width), jnp.float32)] + scratch
    else:
        out_shape = jax.ShapeDtypeStruct((ROWS, width), jnp.float32)
        out_specs = vmem
    return pl.pallas_call(
        functools.partial(aggregate_kernel, plan, offsets, groups, len(sources), first, resident, blocks),
        out_shape=out_shape,
        in_specs=[smem, vmem if resident else hbm] + [vmem] * len(sources) + ([] if first else [vmem]),
        out_specs=out_specs,
        scratch_shapes=scratch,
        compiler_params=pltpu.CompilerParams(vmem_limit_bytes=RESIDENT_LIMIT if resident else STREAM_LIMIT),
        cost_estimate=pl.CostEstimate(
            flops=2 * entries * ROWS * DEPTH * width,
            bytes_accessed=entries * ROWS * DEPTH * 2,
            transcendentals=0,
        ),
        name="aggregate",
    )(need, dense, *sources, *(() if first else (start_total,)))


def product_kernel(blocks, *refs):
    w, out = refs[blocks], refs[blocks + 1]
    width = refs[0].shape[1]
    own = lax.axis_index("feat")
    total = None
    for m in range(blocks):
        rows = pl.ds(pl.multiple_of((own ^ m) * width, width), width)
        term = jnp.dot(refs[m][...], w[rows, :], preferred_element_type=jnp.float32)
        total = term if total is None else total + term
    out[...] = jnp.maximum(total, 0.0).astype(out.dtype)


def product(parts, w):
    blocks = len(parts)
    rows, width = parts[0].shape
    depth, cols = w.shape
    step = 256
    return pl.pallas_call(
        functools.partial(product_kernel, blocks),
        grid=(cols // step,),
        out_shape=jax.ShapeDtypeStruct((rows, cols), jnp.bfloat16),
        in_specs=[pl.BlockSpec((rows, width), lambda j: (0, 0))] * blocks
        + [pl.BlockSpec((depth, step), lambda j: (0, j))],
        out_specs=pl.BlockSpec((rows, step), lambda j: (0, j)),
        compiler_params=pltpu.CompilerParams(vmem_limit_bytes=16 * MIB),
        name="product",
    )(*parts, w)


def slot_table(groups, tile_row, tile_panel, tile_slot, counts):
    slots = lax.iota(jnp.int32, tile_row.shape[0])
    key = (tile_panel * TPP + tile_row) * NEED + tile_slot
    key = jnp.where(slots < counts[0], key, -1)
    places = lax.iota(jnp.int32, groups * PER_PANEL)
    return jnp.max(jnp.where(key[None, :] == places[:, None], slots[None, :] + 1, 0), axis=1)


def group_at(offset, groups):
    own = lax.axis_index("rows")
    place = jnp.where(lax.rem(own, 2) == 0, lax.div(own, 2), groups - 1 - lax.div(own, 2))
    place = lax.rem(place + offset + groups, groups)
    return jnp.where(place < groups // 2, 2 * place, 2 * (groups - 1 - place) + 1)


def needed_rows(need, groups, reader, offset, k):
    tile = need[(group_at(reader, groups) * groups + group_at(offset, groups)) * NEED + k]
    return pl.ds(pl.multiple_of(tile * TILE, TILE), TILE)


def pick_kernel(reader, offset, groups, need, source, out):
    for k in range(NEED):
        out[pl.ds(k * TILE, TILE), :] = source[needed_rows(need, groups, reader, offset, k), :]


def pick(need, source, reader, offset, groups):
    vmem = pl.BlockSpec(memory_space=pltpu.VMEM)
    return pl.pallas_call(
        functools.partial(pick_kernel, reader, offset, groups),
        out_shape=jax.ShapeDtypeStruct((DEPTH, source.shape[1]), source.dtype),
        in_specs=[pl.BlockSpec(memory_space=pltpu.SMEM), vmem],
        out_specs=vmem,
        compiler_params=pltpu.CompilerParams(vmem_limit_bytes=4 * MIB),
        name="pick",
    )(need, source)


def ring_pairs(groups, way):
    order = [2 * p if p < groups // 2 else 2 * (groups - 1 - p) + 1 for p in range(groups)]
    return [(order[p], order[(p + way) % groups]) for p in range(groups)]


def per_device(features, tiles, tile_row, tile_panel, tile_slot, counts, need_list, weight):
    width = features.shape[1]
    groups = lax.axis_size("rows")
    blocks = lax.axis_size("feat")
    far = groups // 2

    def send(array, way):
        return lax.ppermute(array, "rows", ring_pairs(groups, way))

    table = slot_table(groups, tile_row, tile_panel, tile_slot, counts)
    need = need_list.reshape(-1)

    stages = [[0]] + [[-d, d] for d in range(1, far)] + [[far]]

    def is_resident(d):
        return sum(len(stage) for stage in stages[d:]) <= RESIDENT_PANELS

    dense = []
    for d in range(far + 1):
        if d in (0, 2) or is_resident(d) != is_resident(d - 1):
            upto = next((e for e in range(d + 1, far + 1) if e == 2 or is_resident(e) != is_resident(d)), far + 1)
            dense += densify(stages[d:upto], is_resident(d), groups, table, tiles)

    def add(total, d, pieces, final=0):
        plan, sources = [], []
        for entry in pieces:
            column, steps = 0, []
            for array, whole in entry:
                steps.append((len(sources), column, array.shape[1], whole))
                sources.append(array)
                column += array.shape[1]
            plan.append(tuple(steps))
        return aggregate(tuple(plan), stages[d], groups, need, dense[d], is_resident(d), sources, total, width, final)

    cuts = 2 if width % (2 * TILE) == 0 else 1
    part = width // cuts
    long_way = [1, -1][:cuts]
    held = {way: [(features[:, c * part : (c + 1) * part], True) for c in range(cuts)] for way in (1, -1)}
    total = add(None, 0, [[(features, True)]])
    for d in range(1, far + 1):
        fresh = {}
        for c in range(cuts):
            for way in (1, -1):
                last = far if way == long_way[c] else far - 1
                if d > last:
                    continue
                array = held[way][c][0]
                if d == last:
                    array = pick(need, array, way, way - way * d, groups)
                fresh[way, c] = (send(array, way), d < last)
        if d == far:
            break
        for way in (1, -1):
            held[way] = [fresh[way, c] for c in range(cuts)]
        if d > 1:
            total = add(total, d - 1, [before[1], before[-1]])
        before = dict(held)
    total = add(total, far - 1, [before[1], before[-1]])
    parts = add(total, far, [[fresh[long_way[c], c] for c in range(cuts)]], blocks)
    arrived = [parts[0]]
    for m in range(1, blocks):
        arrived.append(lax.ppermute(parts[m], "feat", [(f, f ^ m) for f in range(blocks)]))
    return product(arrived, weight)


def solution(mesh):
    return jax.shard_map(
        per_device,
        mesh=mesh,
        in_specs=(
            P("rows", "feat"),
            P("rows", None, None),
            P("rows"),
            P("rows"),
            P("rows"),
            P("rows"),
            P(),
            P(),
        ),
        out_specs=P(("rows", "feat"), None),
        check_vma=False,
    )
```

```python
import functools

import jax
import jax.numpy as jnp
from jax import lax
from jax.experimental import pallas as pl
from jax.experimental.pallas import tpu as pltpu
from jax.sharding import PartitionSpec as P


TILE = 128
TPP = 16
NEED = 8
PER_PANEL = TPP * NEED
ROWS = TPP * TILE
DEPTH = NEED * TILE
MIB = 1024 * 1024
RESIDENT_PANELS = 8
RESIDENT_LIMIT = 9 * MIB
STREAM_LIMIT = 14 * MIB
DENSIFY_LIMIT = 38 * MIB


def place_tiles(panel, table, tiles, dense, sem):
    base = panel * PER_PANEL

    def row_step(row, found):
        for k in range(NEED):
            slot = table[base + row * NEED + k]
            rows = pl.ds(pl.multiple_of(row * TILE, TILE), TILE)
            cols = pl.ds(k * TILE, TILE)

            @pl.when(slot > 0)
            def _():
                pltpu.make_async_copy(tiles.at[slot - 1], dense.at[rows, cols], sem).start()

            @pl.when(slot == 0)
            def _():
                dense[rows, cols] = jnp.zeros((TILE, TILE), jnp.bfloat16)

            found = found + jnp.where(slot > 0, 1, 0)
        return found

    return lax.fori_loop(0, TPP, row_step, 0)


def await_tiles(found, tiles, dense, sem):
    def wait_one(i, c):
        pltpu.make_async_copy(tiles.at[0], dense.at[pl.ds(0, TILE), pl.ds(0, TILE)], sem).wait()
        return c

    lax.fori_loop(0, found, wait_one, 0)


def densify_kernel(stages, resident, groups, table, tiles, *refs):
    outs, (dense, tile_sem, out_sem) = refs[: len(stages)], refs[len(stages) :]
    entries = [(out, e, o) for out, stage in zip(outs, stages) for e, o in enumerate(stage)]
    if resident:
        found = [
            place_tiles(group_at(o, groups), table, tiles, out.at[e], tile_sem.at[0]) for out, e, o in entries
        ]
        out, e, o = entries[0]
        await_tiles(sum(found), tiles, out.at[e], tile_sem.at[0])
        return
    buffers = dense.shape[0]

    def store(i):
        out, e, _ = entries[i]
        return pltpu.make_async_copy(dense.at[i % buffers], out.at[e], out_sem.at[i % buffers])

    for i, (out, e, o) in enumerate(entries):
        buf = i % buffers
        if i >= buffers:
            store(i - buffers).wait()
        found = place_tiles(group_at(o, groups), table, tiles, dense.at[buf], tile_sem.at[buf])
        await_tiles(found, tiles, dense.at[buf], tile_sem.at[buf])
        store(i).start()
    for i in range(max(0, len(entries) - buffers), len(entries)):
        store(i).wait()


def densify(stages, resident, groups, table, tiles):
    buffers = 1 if resident else 2
    out_space = pltpu.VMEM if resident else pl.ANY
    entries = sum(len(stage) for stage in stages)
    return pl.pallas_call(
        functools.partial(densify_kernel, stages, resident, groups),
        out_shape=[jax.ShapeDtypeStruct((len(stage), ROWS, DEPTH), jnp.bfloat16) for stage in stages],
        in_specs=[pl.BlockSpec(memory_space=pltpu.SMEM), pl.BlockSpec(memory_space=pl.ANY)],
        out_specs=[pl.BlockSpec(memory_space=out_space)] * len(stages),
        scratch_shapes=[
            pltpu.VMEM((8, TILE) if resident else (buffers, ROWS, DEPTH), jnp.bfloat16),
            pltpu.SemaphoreType.DMA((buffers,)),
            pltpu.SemaphoreType.DMA((buffers,)),
        ],
        compiler_params=pltpu.CompilerParams(vmem_limit_bytes=max(10 * MIB, DENSIFY_LIMIT - 2 * entries * ROWS * DEPTH)),
        cost_estimate=pl.CostEstimate(flops=0, bytes_accessed=2 * entries * ROWS * DEPTH, transcendentals=0),
        name="densify",
    )(table, tiles)


def group_at(offset, groups):
    own = lax.axis_index("rows")
    place = jnp.where(lax.rem(own, 2) == 0, lax.div(own, 2), groups - 1 - lax.div(own, 2))
    place = lax.rem(place + offset + groups, groups)
    return jnp.where(place < groups // 2, 2 * place, 2 * (groups - 1 - place) + 1)


def needed_tile(need, groups, reader, offset, k):
    return need[(group_at(reader, groups) * groups + group_at(offset, groups)) * NEED + k]


def gather_feats(need, groups, reader, offset, chunks, whole, put):
    for k in range(NEED):
        if not whole:
            put(k, chunks[0][pl.ds(k * TILE, TILE), :])
            continue
        tile = needed_tile(need, groups, reader, offset, k)
        per_chunk = TPP // len(chunks)
        if len(chunks) == 1:
            put(k, chunks[0][pl.ds(pl.multiple_of(tile * TILE, TILE), TILE), :])
            continue
        for i, chunk in enumerate(chunks):

            @pl.when(lax.div(tile, per_chunk) == i)
            def _():
                row = pl.multiple_of(lax.rem(tile, per_chunk) * TILE, TILE)
                put(k, chunk[pl.ds(row, TILE), :])


def aggregate_kernel(plan, groups, n_sources, n_dense, n_totals, widths, first, blocks, need, *refs):
    sources, refs = refs[:n_sources], refs[n_sources:]
    denses, refs = refs[:n_dense], refs[n_dense:]
    if not first:
        start_totals, refs = refs[:n_totals], refs[n_totals:]
    n_outs = n_totals * max(1, blocks)
    outs, (streamed, feats, *work, sem) = refs[:n_outs], refs[n_outs:]
    totals = work if blocks else outs
    starts = [sum(widths[:t]) for t in range(n_totals)]
    fresh = [first] * n_totals

    for operand, index, resident, offset, pieces in plan:
        if not resident:
            copy = pltpu.make_async_copy(denses[operand].at[index], streamed, sem)
            copy.start()
        for part, chunks, whole in pieces:
            cols = pl.ds(starts[part], widths[part])

            def put(k, value):
                feats[pl.ds(k * TILE, TILE), cols] = value

            gather_feats(need, groups, 0, offset, [sources[i] for i in chunks], whole, put)
        if not resident:
            copy.wait()
        lhs = denses[operand][index] if resident else streamed[...]
        parts = [part for part, chunks, whole in pieces]
        low, high = starts[parts[0]], starts[parts[-1]] + widths[parts[-1]]
        term = jnp.dot(lhs, feats[:, low:high], preferred_element_type=jnp.float32)
        for part in parts:
            piece = term[:, starts[part] - low : starts[part] - low + widths[part]]
            if fresh[part]:
                totals[part][...] = piece
            elif plan_first(plan, part) == (operand, index):
                totals[part][...] = start_totals[part][...] + piece
            else:
                totals[part][...] += piece
            fresh[part] = False
    for part in range(n_totals):
        if not first and plan_first(plan, part) is None:
            totals[part][...] = start_totals[part][...]
    if blocks:
        own = lax.axis_index("feat")
        size = ROWS // blocks
        for part in range(n_totals):
            for m in range(blocks):
                rows = pl.ds(pl.multiple_of((own ^ m) * size, size), size)
                outs[part * blocks + m][...] = totals[part][rows, :].astype(jnp.bfloat16)


def plan_first(plan, part):
    for operand, index, resident, offset, pieces in plan:
        if any(piece[0] == part for piece in pieces):
            return (operand, index)
    return None


def aggregate(plan, groups, need, sources, denses, totals, widths, blocks=0):
    first = totals is None
    n_totals = len(widths)
    smem = pl.BlockSpec(memory_space=pltpu.SMEM)
    vmem = pl.BlockSpec(memory_space=pltpu.VMEM)
    spaces = [None] * len(denses)
    for operand, index, resident, offset, pieces in plan:
        spaces[operand] = vmem if resident else pl.BlockSpec(memory_space=pl.ANY)
    streams = any(not entry[2] for entry in plan)
    scratch = [
        pltpu.VMEM((ROWS, DEPTH) if streams else (8, TILE), jnp.bfloat16),
        pltpu.VMEM((DEPTH, sum(widths)), jnp.bfloat16),
    ]
    if blocks:
        out_shape = [jax.ShapeDtypeStruct((ROWS // blocks, w), jnp.bfloat16) for w in widths for _ in range(blocks)]
        scratch += [pltpu.VMEM((ROWS, w), jnp.float32) for w in widths]
    else:
        out_shape = [jax.ShapeDtypeStruct((ROWS, w), jnp.float32) for w in widths]
    flops = sum(2 * ROWS * DEPTH * sum(widths[p[0]] for p in entry[4]) for entry in plan)
    return pl.pallas_call(
        functools.partial(
            aggregate_kernel, plan, groups, len(sources), len(denses), n_totals, widths, first, blocks
        ),
        out_shape=out_shape,
        in_specs=[smem] + [vmem] * len(sources) + spaces + ([] if first else [vmem] * n_totals),
        out_specs=[vmem] * len(out_shape),
        scratch_shapes=scratch + [pltpu.SemaphoreType.DMA],
        compiler_params=pltpu.CompilerParams(vmem_limit_bytes=STREAM_LIMIT if streams else RESIDENT_LIMIT),
        cost_estimate=pl.CostEstimate(
            flops=flops, bytes_accessed=len(plan) * ROWS * DEPTH * 2, transcendentals=0
        ),
        name="aggregate",
    )(need, *sources, *denses, *([] if first else totals))


def pick_kernel(reader, offset, groups, need, *refs):
    chunks, out = refs[:-1], refs[-1]

    def put(k, value):
        out[pl.ds(k * TILE, TILE), :] = value

    gather_feats(need, groups, reader, offset, chunks, True, put)


def pick(need, chunks, reader, offset, groups):
    vmem = pl.BlockSpec(memory_space=pltpu.VMEM)
    return pl.pallas_call(
        functools.partial(pick_kernel, reader, offset, groups),
        out_shape=jax.ShapeDtypeStruct((DEPTH, chunks[0].shape[1]), chunks[0].dtype),
        in_specs=[pl.BlockSpec(memory_space=pltpu.SMEM)] + [vmem] * len(chunks),
        out_specs=vmem,
        compiler_params=pltpu.CompilerParams(vmem_limit_bytes=4 * MIB),
        name="pick",
    )(need, *chunks)


def product_kernel(terms, starts, shard, last, w, *refs):
    parts, refs = refs[:terms], refs[terms:]
    own = lax.axis_index("feat")
    total = None if last is None else refs[0][...]
    out = refs[-1]
    for i in range(0, terms, 2):
        pair = range(i, min(i + 2, terms))
        x = jnp.concatenate([parts[j][...] for j in pair], axis=1)
        rows = []
        for j in pair:
            m, column = starts[j]
            row = pl.multiple_of((own ^ m) * shard + column, TILE)
            rows.append(w[pl.ds(row, parts[j].shape[1]), :])
        term = jnp.dot(x, jnp.concatenate(rows, axis=0), preferred_element_type=jnp.float32)
        total = term if total is None else total + term
    out[...] = total if out.dtype == jnp.float32 else jnp.maximum(total, 0.0).astype(out.dtype)


def product(operands, starts, shard, w, start_total, dtype):
    rows = operands[0].shape[0]
    depth, cols = w.shape
    step = 256
    vmem = pl.BlockSpec(memory_space=pltpu.VMEM)
    band = pl.BlockSpec((rows, step), lambda j: (0, j))
    first = start_total is None
    return pl.pallas_call(
        functools.partial(product_kernel, len(operands), starts, shard, None if first else 0),
        grid=(cols // step,),
        out_shape=jax.ShapeDtypeStruct((rows, cols), dtype),
        in_specs=[pl.BlockSpec((depth, step), lambda j: (0, j))]
        + [pl.BlockSpec(x.shape, lambda j: (0, 0)) for x in operands]
        + ([] if first else [band]),
        out_specs=band,
        compiler_params=pltpu.CompilerParams(vmem_limit_bytes=16 * MIB),
        cost_estimate=pl.CostEstimate(
            flops=2 * rows * cols * sum(x.shape[1] for x in operands), bytes_accessed=8 * rows * cols, transcendentals=0
        ),
        name="product",
    )(w, *operands, *([] if first else [start_total]))


def slot_table(groups, tile_row, tile_panel, tile_slot, counts):
    slots = lax.iota(jnp.int32, tile_row.shape[0])
    key = (tile_panel * TPP + tile_row) * NEED + tile_slot
    key = jnp.where(slots < counts[0], key, -1)
    places = lax.iota(jnp.int32, groups * PER_PANEL)
    return jnp.max(jnp.where(key[None, :] == places[:, None], slots[None, :] + 1, 0), axis=1)


def ring_pairs(groups, way):
    order = [2 * p if p < groups // 2 else 2 * (groups - 1 - p) + 1 for p in range(groups)]
    return [(order[p], order[(p + way) % groups]) for p in range(groups)]


def per_device(features, tiles, tile_row, tile_panel, tile_slot, counts, need_list, weight):
    width = features.shape[1]
    groups = lax.axis_size("rows")
    blocks = lax.axis_size("feat")
    far = groups // 2
    cuts = part_count(width)
    part = width // cuts
    widths = (part,) * cuts
    last = cuts - 1
    need = need_list.reshape(-1)

    def send(array, way):
        return lax.ppermute(array, "rows", ring_pairs(groups, way))

    held = {}
    for c in range(cuts):
        column = features[:, c * part : (c + 1) * part]
        for way in (1, -1):
            n = chunk_count(way, c)
            held[way, 0, c] = ([column[i * ROWS // n : (i + 1) * ROWS // n] for i in range(n)], True)
    for d in range(1, far + 1):
        for c in range(cuts):
            for way in (1, -1):
                end = hop_end(way, c, far)
                chunks = held.get((way, d - 1, c), (None,))[0]
                if d < end:
                    held[way, d, c] = ([send(x, way) for x in chunks], True)
                elif d == end:
                    chosen = pick(need, chunks, way, way - way * d, groups)
                    held[way, d, c] = ([send(chosen, way)], False)

    table = slot_table(groups, tile_row, tile_panel, tile_slot, counts)
    stages = [[0]] + [[-d, d] for d in range(1, far)] + [[far]]

    def is_resident(d):
        return sum(len(stage) for stage in stages[d:]) <= RESIDENT_PANELS

    dense = []
    for d in range(far + 1):
        if d in (0, 2) or is_resident(d) != is_resident(d - 1):
            upto = next((e for e in range(d + 1, far + 1) if e == 2 or is_resident(e) != is_resident(d)), far + 1)
            dense += densify(stages[d:upto], is_resident(d), groups, table, tiles)

    def add(totals, entries, columns, final=0):
        sources, operands, plan = [], [], []
        for way, d, parts in entries:
            if d not in operands:
                operands.append(d)
            offset = -way * d
            pieces = []
            for c in parts:
                chunks, whole = held[-1 if d == 0 else way, d, c]
                pieces.append((columns.index(c), tuple(range(len(sources), len(sources) + len(chunks))), whole))
                sources += chunks
            index = stages[d].index(offset) if d < far else 0
            plan.append((operands.index(d), index, is_resident(d), offset, tuple(pieces)))
        sizes = tuple(widths[c] for c in columns)
        return aggregate(tuple(plan), groups, need, sources, [dense[d] for d in operands], totals, sizes, final)

    every = list(range(cuts))
    totals = add(None, [(1, 0, every)], every)
    for d in range(1, far - 2):
        totals = add(totals, [(1, d, every), (-1, d, every)], every)
    d = far - 2
    if cuts > 1:
        early = [(-1, d, every), (1, d, [0]), (1, d + 1, [0])]
        totals = add(totals, early, every)
        rest = add([totals[1]], [(1, d, [1]), (-1, d + 1, [1])], [1])
        ends = [
            add([totals[0]], [(-1, d + 1, [0]), (1, far, [0])], [0], blocks),
            add(rest, [(1, d + 1, [1]), (-1, far, [1])], [1], blocks),
        ]
    else:
        totals = add(totals, [(1, d, every), (-1, d, every)], every)
        totals = add(totals, [(1, d + 1, every), (-1, d + 1, every)], every)
        ends = [add(totals, [(1, far, every)], every, blocks)]

    def exchange(c, m):
        if m == 0:
            return ends[c][0]
        return lax.ppermute(ends[c][m], "feat", [(f, f ^ m) for f in range(blocks)])

    order = [(c, m) for c in range(cuts) for m in reversed(range(blocks))]
    arrived = {key: exchange(*key) for key in order}
    late = [(last, m) for m in range(2, blocks)]
    soon = [(c, m) for m in range(blocks) for c in range(cuts) if (c, m) not in late]

    def multiply(keys, start_total, dtype):
        starts = tuple((m, c * part) for c, m in keys)
        return product([arrived[key] for key in keys], starts, width, weight, start_total, dtype)

    if not late:
        return multiply(soon, None, jnp.bfloat16)
    return multiply(late, multiply(soon, None, jnp.float32), jnp.bfloat16)


def part_count(width):
    return 2 if width % (2 * TILE) == 0 else 1


def chunk_count(way, c):
    return 2 if way > 0 and c == 1 else 1


def hop_end(way, c, far):
    return far if (way > 0) == (c == 0) else far - 1


def solution(mesh):
    return jax.shard_map(
        per_device,
        mesh=mesh,
        in_specs=(
            P("rows", "feat"),
            P("rows", None, None),
            P("rows"),
            P("rows"),
            P("rows"),
            P("rows"),
            P(),
            P(),
        ),
        out_specs=P(("rows", "feat"), None),
        check_vma=False,
    )
```

```python
import functools

import jax
import jax.numpy as jnp
from jax import lax
from jax.experimental import pallas as pl
from jax.experimental.pallas import tpu as pltpu
from jax.sharding import PartitionSpec as P


TILE = 128
TPP = 16
NEED = 8
PER_PANEL = TPP * NEED
ROWS = TPP * TILE
DEPTH = NEED * TILE
MIB = 1024 * 1024
RESIDENT_PANELS = 8
RESIDENT_LIMIT = 9 * MIB
STREAM_LIMIT = 14 * MIB
DENSIFY_LIMIT = 38 * MIB


def place_tiles(panel, table, tiles, dense, sem):
    base = panel * PER_PANEL

    def row_step(row, found):
        for k in range(NEED):
            slot = table[base + row * NEED + k]
            rows = pl.ds(pl.multiple_of(row * TILE, TILE), TILE)
            cols = pl.ds(k * TILE, TILE)

            @pl.when(slot > 0)
            def _():
                pltpu.make_async_copy(tiles.at[slot - 1], dense.at[rows, cols], sem).start()

            @pl.when(slot == 0)
            def _():
                dense[rows, cols] = jnp.zeros((TILE, TILE), jnp.bfloat16)

            found = found + jnp.where(slot > 0, 1, 0)
        return found

    return lax.fori_loop(0, TPP, row_step, 0)


def await_tiles(found, tiles, dense, sem):
    def wait_one(i, c):
        pltpu.make_async_copy(tiles.at[0], dense.at[pl.ds(0, TILE), pl.ds(0, TILE)], sem).wait()
        return c

    lax.fori_loop(0, found, wait_one, 0)


def densify_kernel(stages, resident, groups, table, tiles, *refs):
    outs, (dense, tile_sem, out_sem) = refs[: len(stages)], refs[len(stages) :]
    entries = [(out, e, o) for out, stage in zip(outs, stages) for e, o in enumerate(stage)]
    if resident:
        found = [
            place_tiles(group_at(o, groups), table, tiles, out.at[e], tile_sem.at[0]) for out, e, o in entries
        ]
        out, e, o = entries[0]
        await_tiles(sum(found), tiles, out.at[e], tile_sem.at[0])
        return
    buffers = dense.shape[0]

    def store(i):
        out, e, _ = entries[i]
        return pltpu.make_async_copy(dense.at[i % buffers], out.at[e], out_sem.at[i % buffers])

    for i, (out, e, o) in enumerate(entries):
        buf = i % buffers
        if i >= buffers:
            store(i - buffers).wait()
        found = place_tiles(group_at(o, groups), table, tiles, dense.at[buf], tile_sem.at[buf])
        await_tiles(found, tiles, dense.at[buf], tile_sem.at[buf])
        store(i).start()
    for i in range(max(0, len(entries) - buffers), len(entries)):
        store(i).wait()


def densify(stages, resident, groups, table, tiles):
    buffers = 1 if resident else 2
    out_space = pltpu.VMEM if resident else pl.ANY
    entries = sum(len(stage) for stage in stages)
    return pl.pallas_call(
        functools.partial(densify_kernel, stages, resident, groups),
        out_shape=[jax.ShapeDtypeStruct((len(stage), ROWS, DEPTH), jnp.bfloat16) for stage in stages],
        in_specs=[pl.BlockSpec(memory_space=pltpu.SMEM), pl.BlockSpec(memory_space=pl.ANY)],
        out_specs=[pl.BlockSpec(memory_space=out_space)] * len(stages),
        scratch_shapes=[
            pltpu.VMEM((8, TILE) if resident else (buffers, ROWS, DEPTH), jnp.bfloat16),
            pltpu.SemaphoreType.DMA((buffers,)),
            pltpu.SemaphoreType.DMA((buffers,)),
        ],
        compiler_params=pltpu.CompilerParams(vmem_limit_bytes=max(10 * MIB, DENSIFY_LIMIT - 2 * entries * ROWS * DEPTH)),
        cost_estimate=pl.CostEstimate(flops=0, bytes_accessed=2 * entries * ROWS * DEPTH, transcendentals=0),
        name="densify",
    )(table, tiles)


def group_at(offset, groups):
    own = lax.axis_index("rows")
    place = jnp.where(lax.rem(own, 2) == 0, lax.div(own, 2), groups - 1 - lax.div(own, 2))
    place = lax.rem(place + offset + groups, groups)
    return jnp.where(place < groups // 2, 2 * place, 2 * (groups - 1 - place) + 1)


def needed_tile(need, groups, reader, offset, k):
    return need[(group_at(reader, groups) * groups + group_at(offset, groups)) * NEED + k]


def gather_feats(need, groups, reader, offset, chunks, whole, put):
    for k in range(NEED):
        if not whole:
            put(k, chunks[0][pl.ds(k * TILE, TILE), :])
            continue
        tile = needed_tile(need, groups, reader, offset, k)
        per_chunk = TPP // len(chunks)
        if len(chunks) == 1:
            put(k, chunks[0][pl.ds(pl.multiple_of(tile * TILE, TILE), TILE), :])
            continue
        for i, chunk in enumerate(chunks):

            @pl.when(lax.div(tile, per_chunk) == i)
            def _():
                row = pl.multiple_of(lax.rem(tile, per_chunk) * TILE, TILE)
                put(k, chunk[pl.ds(row, TILE), :])


def aggregate_kernel(plan, groups, n_sources, n_dense, n_totals, widths, first, need, *refs):
    sources, refs = refs[:n_sources], refs[n_sources:]
    denses, refs = refs[:n_dense], refs[n_dense:]
    if not first:
        start_totals, refs = refs[:n_totals], refs[n_totals:]
    totals, (streamed, feats, sem) = refs[:n_totals], refs[n_totals:]
    starts = [sum(widths[:t]) for t in range(n_totals)]
    fresh = [first] * n_totals

    for operand, index, resident, offset, pieces in plan:
        if not resident:
            copy = pltpu.make_async_copy(denses[operand].at[index], streamed, sem)
            copy.start()
        for part, chunks, whole in pieces:
            cols = pl.ds(starts[part], widths[part])

            def put(k, value):
                feats[pl.ds(k * TILE, TILE), cols] = value

            gather_feats(need, groups, 0, offset, [sources[i] for i in chunks], whole, put)
        if not resident:
            copy.wait()
        lhs = denses[operand][index] if resident else streamed[...]
        parts = [part for part, chunks, whole in pieces]
        low, high = starts[parts[0]], starts[parts[-1]] + widths[parts[-1]]
        term = jnp.dot(lhs, feats[:, low:high], preferred_element_type=jnp.float32)
        for part in parts:
            piece = term[:, starts[part] - low : starts[part] - low + widths[part]]
            if fresh[part]:
                totals[part][...] = piece
            elif plan_first(plan, part) == (operand, index):
                totals[part][...] = start_totals[part][...] + piece
            else:
                totals[part][...] += piece
            fresh[part] = False
    for part in range(n_totals):
        if not first and plan_first(plan, part) is None:
            totals[part][...] = start_totals[part][...]


def finish_kernel(plan, groups, n_sources, n_dense, blocks, pairs, need, *refs):
    sources, refs = refs[:n_sources], refs[n_sources:]
    denses, refs = refs[:n_dense], refs[n_dense:]
    start_total, refs = refs[0], refs[1:]
    outs, (streamed, feats, total, sem) = refs[: 2 * len(pairs)], refs[2 * len(pairs) :]
    own = lax.axis_index("feat")
    size = ROWS // blocks
    for e, (operand, index, resident, offset, pieces) in enumerate(plan):
        ((part, chunks, whole),) = pieces

        def put(k, value):
            feats[e, pl.ds(k * TILE, TILE), :] = value

        gather_feats(need, groups, 0, offset, [sources[i] for i in chunks], whole, put)
    for i, pair in enumerate(pairs):
        rows = pl.ds(pl.multiple_of((lax.div(own, 2) ^ pair) * 2 * size, 2 * size), 2 * size)
        total[...] = start_total[rows, :]
        for e, (operand, index, resident, offset, pieces) in enumerate(plan):
            if resident:
                lhs = denses[operand][index, rows, :]
            else:
                copy = pltpu.make_async_copy(denses[operand].at[index, rows, :], streamed, sem)
                copy.start()
                copy.wait()
                lhs = streamed[...]
            total[...] += jnp.dot(lhs, feats[e], preferred_element_type=jnp.float32)
        for low in range(2):
            block = pl.ds(pl.multiple_of((lax.rem(own, 2) ^ low) * size, size), size)
            outs[2 * i + low][...] = total[block, :].astype(jnp.bfloat16)


def finish(plan, groups, need, sources, denses, start_total, blocks, pairs):
    width = start_total.shape[1]
    vmem = pl.BlockSpec(memory_space=pltpu.VMEM)
    spaces = [None] * len(denses)
    for operand, index, resident, offset, pieces in plan:
        spaces[operand] = vmem if resident else pl.BlockSpec(memory_space=pl.ANY)
    streams = any(not entry[2] for entry in plan)
    rows = 2 * ROWS // blocks
    return pl.pallas_call(
        functools.partial(finish_kernel, plan, groups, len(sources), len(denses), blocks, pairs),
        out_shape=[jax.ShapeDtypeStruct((ROWS // blocks, width), jnp.bfloat16)] * (2 * len(pairs)),
        in_specs=[pl.BlockSpec(memory_space=pltpu.SMEM)] + [vmem] * len(sources) + spaces + [vmem],
        out_specs=[vmem] * (2 * len(pairs)),
        scratch_shapes=[
            pltpu.VMEM((rows, DEPTH) if streams else (8, TILE), jnp.bfloat16),
            pltpu.VMEM((len(plan), DEPTH, width), jnp.bfloat16),
            pltpu.VMEM((rows, width), jnp.float32),
            pltpu.SemaphoreType.DMA,
        ],
        compiler_params=pltpu.CompilerParams(vmem_limit_bytes=STREAM_LIMIT if streams else RESIDENT_LIMIT),
        cost_estimate=pl.CostEstimate(
            flops=2 * len(plan) * len(pairs) * rows * DEPTH * width,
            bytes_accessed=2 * len(plan) * len(pairs) * rows * DEPTH,
            transcendentals=0,
        ),
        name="finish",
    )(need, *sources, *denses, start_total)


def plan_first(plan, part):
    for operand, index, resident, offset, pieces in plan:
        if any(piece[0] == part for piece in pieces):
            return (operand, index)
    return None


def aggregate(plan, groups, need, sources, denses, totals, widths):
    first = totals is None
    n_totals = len(widths)
    smem = pl.BlockSpec(memory_space=pltpu.SMEM)
    vmem = pl.BlockSpec(memory_space=pltpu.VMEM)
    spaces = [None] * len(denses)
    for operand, index, resident, offset, pieces in plan:
        spaces[operand] = vmem if resident else pl.BlockSpec(memory_space=pl.ANY)
    streams = any(not entry[2] for entry in plan)
    scratch = [
        pltpu.VMEM((ROWS, DEPTH) if streams else (8, TILE), jnp.bfloat16),
        pltpu.VMEM((DEPTH, sum(widths)), jnp.bfloat16),
    ]
    out_shape = [jax.ShapeDtypeStruct((ROWS, w), jnp.float32) for w in widths]
    flops = sum(2 * ROWS * DEPTH * sum(widths[p[0]] for p in entry[4]) for entry in plan)
    return pl.pallas_call(
        functools.partial(
            aggregate_kernel, plan, groups, len(sources), len(denses), n_totals, widths, first
        ),
        out_shape=out_shape,
        in_specs=[smem] + [vmem] * len(sources) + spaces + ([] if first else [vmem] * n_totals),
        out_specs=[vmem] * len(out_shape),
        scratch_shapes=scratch + [pltpu.SemaphoreType.DMA],
        compiler_params=pltpu.CompilerParams(vmem_limit_bytes=STREAM_LIMIT if streams else RESIDENT_LIMIT),
        cost_estimate=pl.CostEstimate(
            flops=flops, bytes_accessed=len(plan) * ROWS * DEPTH * 2, transcendentals=0
        ),
        name="aggregate",
    )(need, *sources, *denses, *([] if first else totals))


def pick_kernel(reader, offset, groups, need, *refs):
    chunks, out = refs[:-1], refs[-1]

    def put(k, value):
        out[pl.ds(k * TILE, TILE), :] = value

    gather_feats(need, groups, reader, offset, chunks, True, put)


def pick(need, chunks, reader, offset, groups):
    vmem = pl.BlockSpec(memory_space=pltpu.VMEM)
    return pl.pallas_call(
        functools.partial(pick_kernel, reader, offset, groups),
        out_shape=jax.ShapeDtypeStruct((DEPTH, chunks[0].shape[1]), chunks[0].dtype),
        in_specs=[pl.BlockSpec(memory_space=pltpu.SMEM)] + [vmem] * len(chunks),
        out_specs=vmem,
        compiler_params=pltpu.CompilerParams(vmem_limit_bytes=4 * MIB),
        name="pick",
    )(need, *chunks)


def product_kernel(terms, starts, shard, first, final, w, *refs):
    parts, refs = refs[:terms], refs[terms:]
    start_total, refs = (None, refs) if first else (refs[0], refs[1:])
    own = lax.axis_index("feat")
    cols = w.shape[1]
    step = 2 * TILE

    def write(j):
        return pltpu.make_async_copy(refs[1].at[j], refs[0].at[:, pl.ds(j * step, step)], refs[2].at[j])

    for j in range(cols // step):
        band = pl.ds(j * step, step)
        total = None if first else start_total[:, band]
        for i in range(0, terms, 2):
            pair = range(i, min(i + 2, terms))
            x = jnp.concatenate([parts[t][...] for t in pair], axis=1)
            rows = []
            for t in pair:
                m, column = starts[t]
                row = pl.multiple_of((own ^ m) * shard + column, TILE)
                rows.append(w[pl.ds(row, parts[t].shape[1]), band])
            term = jnp.dot(x, jnp.concatenate(rows, axis=0), preferred_element_type=jnp.float32)
            total = term if total is None else total + term
        if final:
            refs[1][j] = jnp.maximum(total, 0.0).astype(jnp.bfloat16)
            write(j).start()
        else:
            refs[0][:, band] = total
    if final:
        for j in range(cols // step):
            write(j).wait()


def product(operands, starts, shard, w, start_total, final):
    rows = operands[0].shape[0]
    _, cols = w.shape
    bands = cols // (2 * TILE)
    vmem = pl.BlockSpec(memory_space=pltpu.VMEM)
    first = start_total is None
    scratch = [pltpu.VMEM((bands, rows, 2 * TILE), jnp.bfloat16), pltpu.SemaphoreType.DMA((bands,))]
    return pl.pallas_call(
        functools.partial(product_kernel, len(operands), starts, shard, first, final),
        out_shape=jax.ShapeDtypeStruct((rows, cols), jnp.bfloat16 if final else jnp.float32),
        in_specs=[vmem] * (1 + len(operands) + (0 if first else 1)),
        out_specs=pl.BlockSpec(memory_space=pl.ANY) if final else vmem,
        scratch_shapes=scratch if final else [],
        compiler_params=pltpu.CompilerParams(vmem_limit_bytes=10 * MIB),
        cost_estimate=pl.CostEstimate(
            flops=2 * rows * cols * sum(x.shape[1] for x in operands), bytes_accessed=8 * rows * cols, transcendentals=0
        ),
        name="product",
    )(w, *operands, *([] if first else [start_total]))


def slot_table(groups, tile_row, tile_panel, tile_slot, counts):
    slots = lax.iota(jnp.int32, tile_row.shape[0])
    key = (tile_panel * TPP + tile_row) * NEED + tile_slot
    key = jnp.where(slots < counts[0], key, -1)
    places = lax.iota(jnp.int32, groups * PER_PANEL)
    return jnp.max(jnp.where(key[None, :] == places[:, None], slots[None, :] + 1, 0), axis=1)


def ring_pairs(groups, way):
    order = [2 * p if p < groups // 2 else 2 * (groups - 1 - p) + 1 for p in range(groups)]
    return [(order[p], order[(p + way) % groups]) for p in range(groups)]


def per_device(features, tiles, tile_row, tile_panel, tile_slot, counts, need_list, weight):
    width = features.shape[1]
    groups = lax.axis_size("rows")
    blocks = lax.axis_size("feat")
    far = groups // 2
    cuts = part_count(width)
    part = width // cuts
    widths = (part,) * cuts
    last = cuts - 1
    need = need_list.reshape(-1)

    def send(array, way):
        return lax.ppermute(array, "rows", ring_pairs(groups, way))

    held = {}
    for c in range(cuts):
        column = features[:, c * part : (c + 1) * part]
        for way in (1, -1):
            n = chunk_count(way, c)
            held[way, 0, c] = ([column[i * ROWS // n : (i + 1) * ROWS // n] for i in range(n)], True)
    for d in range(1, far + 1):
        for c in range(cuts):
            for way in (1, -1):
                end = hop_end(way, c, far)
                chunks = held.get((way, d - 1, c), (None,))[0]
                if d < end:
                    held[way, d, c] = ([send(x, way) for x in chunks], True)
                elif d == end:
                    chosen = pick(need, chunks, way, way - way * d, groups)
                    held[way, d, c] = ([send(chosen, way)], False)

    table = slot_table(groups, tile_row, tile_panel, tile_slot, counts)
    stages = [[0]] + [[-d, d] for d in range(1, far)] + [[far]]

    def is_resident(d):
        return sum(len(stage) for stage in stages[d:]) <= RESIDENT_PANELS

    dense = []
    for d in range(far + 1):
        if d in (0, 2) or is_resident(d) != is_resident(d - 1):
            upto = next((e for e in range(d + 1, far + 1) if e == 2 or is_resident(e) != is_resident(d)), far + 1)
            dense += densify(stages[d:upto], is_resident(d), groups, table, tiles)

    def add(totals, entries, columns, pairs=None):
        sources, operands, plan = [], [], []
        for way, d, parts in entries:
            if d not in operands:
                operands.append(d)
            offset = -way * d
            pieces = []
            for c in parts:
                chunks, whole = held[-1 if d == 0 else way, d, c]
                pieces.append((columns.index(c), tuple(range(len(sources), len(sources) + len(chunks))), whole))
                sources += chunks
            index = stages[d].index(offset) if d < far else 0
            plan.append((operands.index(d), index, is_resident(d), offset, tuple(pieces)))
        sizes = tuple(widths[c] for c in columns)
        if pairs is not None:
            arrays = [dense[d] for d in operands]
            return finish(tuple(plan), groups, need, sources, arrays, totals[0], blocks, pairs)
        return aggregate(tuple(plan), groups, need, sources, [dense[d] for d in operands], totals, sizes)

    every = list(range(cuts))
    totals = add(None, [(1, 0, every)], every)
    for d in range(1, far - 2):
        totals = add(totals, [(1, d, every), (-1, d, every)], every)
    d = far - 2
    if cuts > 1:
        early = [(-1, d, every), (1, d, [0]), (1, d + 1, [0])]
        totals = add(totals, early, every)
        rest = add([totals[1]], [(1, d, [1]), (-1, d + 1, [1])], [1])
        ends = [
            (totals[0], [(-1, d + 1, [0]), (1, far, [0])]),
            (rest[0], [(1, d + 1, [1]), (-1, far, [1])]),
        ]
    else:
        totals = add(totals, [(1, d, every), (-1, d, every)], every)
        totals = add(totals, [(1, d + 1, every), (-1, d + 1, every)], every)
        ends = [(totals[0], [(1, far, every)])]

    finished = {}
    for c, (total, entries) in enumerate(ends):
        for pairs in (tuple(range(1, blocks // 2)), (0,)):
            for pair, outs in zip(pairs, halves(add([total], entries, [c], pairs) if pairs else [])):
                finished[c, 2 * pair], finished[c, 2 * pair + 1] = outs

    def exchange(c, m):
        if m == 0:
            return finished[c, 0]
        return lax.ppermute(finished[c, m], "feat", [(f, f ^ m) for f in range(blocks)])

    order = [(c, m) for c in range(cuts) for m in reversed(range(blocks))]
    arrived = {key: exchange(*key) for key in order}
    late = [(last, m) for m in range(2, blocks)]
    soon = [(c, m) for m in range(blocks) for c in range(cuts) if (c, m) not in late]

    def multiply(keys, start_total, final):
        starts = tuple((m, c * part) for c, m in keys)
        return product([arrived[key] for key in keys], starts, width, weight, start_total, final)

    if not late:
        return multiply(soon, None, True)
    return multiply(late, multiply(soon, None, False), True)


def halves(outs):
    return [(outs[i], outs[i + 1]) for i in range(0, len(outs), 2)]


def part_count(width):
    return 2 if width % (2 * TILE) == 0 else 1


def chunk_count(way, c):
    return 2 if way > 0 and c == 1 else 1


def hop_end(way, c, far):
    return far if (way > 0) == (c == 0) else far - 1


def solution(mesh):
    return jax.shard_map(
        per_device,
        mesh=mesh,
        in_specs=(
            P("rows", "feat"),
            P("rows", None, None),
            P("rows"),
            P("rows"),
            P("rows"),
            P("rows"),
            P(),
            P(),
        ),
        out_specs=P(("rows", "feat"), None),
        check_vma=False,
    )
```

```python
import functools

import jax
import jax.numpy as jnp
from jax import lax
from jax.experimental import pallas as pl
from jax.experimental.pallas import tpu as pltpu
from jax.sharding import PartitionSpec as P


TILE = 128
TPP = 16
NEED = 8
PER_PANEL = TPP * NEED
ROWS = TPP * TILE
DEPTH = NEED * TILE
MIB = 1024 * 1024
RESIDENT_PANELS = 8
RESIDENT_LIMIT = 9 * MIB
STREAM_LIMIT = 14 * MIB
DENSIFY_LIMIT = 38 * MIB


def place_tiles(panel, table, tiles, dense, sem):
    base = panel * PER_PANEL

    def row_step(row, found):
        for k in range(NEED):
            slot = table[base + row * NEED + k]
            rows = pl.ds(pl.multiple_of(row * TILE, TILE), TILE)
            cols = pl.ds(k * TILE, TILE)

            @pl.when(slot > 0)
            def _():
                pltpu.make_async_copy(tiles.at[slot - 1], dense.at[rows, cols], sem).start()

            @pl.when(slot == 0)
            def _():
                dense[rows, cols] = jnp.zeros((TILE, TILE), jnp.bfloat16)

            found = found + jnp.where(slot > 0, 1, 0)
        return found

    return lax.fori_loop(0, TPP, row_step, 0)


def await_tiles(found, tiles, dense, sem):
    def wait_one(i, c):
        pltpu.make_async_copy(tiles.at[0], dense.at[pl.ds(0, TILE), pl.ds(0, TILE)], sem).wait()
        return c

    lax.fori_loop(0, found, wait_one, 0)


def densify_kernel(stages, resident, groups, table, tiles, *refs):
    outs, (dense, tile_sem, out_sem) = refs[: len(stages)], refs[len(stages) :]
    entries = [(out, e, o) for out, stage in zip(outs, stages) for e, o in enumerate(stage)]
    if resident:
        found = [
            place_tiles(group_at(o, groups), table, tiles, out.at[e], tile_sem.at[0]) for out, e, o in entries
        ]
        out, e, o = entries[0]
        await_tiles(sum(found), tiles, out.at[e], tile_sem.at[0])
        return
    buffers = dense.shape[0]

    def store(i):
        out, e, _ = entries[i]
        return pltpu.make_async_copy(dense.at[i % buffers], out.at[e], out_sem.at[i % buffers])

    for i, (out, e, o) in enumerate(entries):
        buf = i % buffers
        if i >= buffers:
            store(i - buffers).wait()
        found = place_tiles(group_at(o, groups), table, tiles, dense.at[buf], tile_sem.at[buf])
        await_tiles(found, tiles, dense.at[buf], tile_sem.at[buf])
        store(i).start()
    for i in range(max(0, len(entries) - buffers), len(entries)):
        store(i).wait()


def densify(stages, resident, groups, table, tiles):
    buffers = 1 if resident else 2
    out_space = pltpu.VMEM if resident else pl.ANY
    entries = sum(len(stage) for stage in stages)
    return pl.pallas_call(
        functools.partial(densify_kernel, stages, resident, groups),
        out_shape=[jax.ShapeDtypeStruct((len(stage), ROWS, DEPTH), jnp.bfloat16) for stage in stages],
        in_specs=[pl.BlockSpec(memory_space=pltpu.SMEM), pl.BlockSpec(memory_space=pl.ANY)],
        out_specs=[pl.BlockSpec(memory_space=out_space)] * len(stages),
        scratch_shapes=[
            pltpu.VMEM((8, TILE) if resident else (buffers, ROWS, DEPTH), jnp.bfloat16),
            pltpu.SemaphoreType.DMA((buffers,)),
            pltpu.SemaphoreType.DMA((buffers,)),
        ],
        compiler_params=pltpu.CompilerParams(vmem_limit_bytes=max(10 * MIB, DENSIFY_LIMIT - 2 * entries * ROWS * DEPTH)),
        cost_estimate=pl.CostEstimate(flops=0, bytes_accessed=2 * entries * ROWS * DEPTH, transcendentals=0),
        name="densify",
    )(table, tiles)


def group_at(offset, groups):
    own = lax.axis_index("rows")
    place = jnp.where(lax.rem(own, 2) == 0, lax.div(own, 2), groups - 1 - lax.div(own, 2))
    place = lax.rem(place + offset + groups, groups)
    return jnp.where(place < groups // 2, 2 * place, 2 * (groups - 1 - place) + 1)


def needed_tile(need, groups, reader, offset, k):
    return need[(group_at(reader, groups) * groups + group_at(offset, groups)) * NEED + k]


def gather_feats(need, groups, reader, offset, chunks, whole, put):
    for k in range(NEED):
        if not whole:
            put(k, chunks[0][pl.ds(k * TILE, TILE), :])
            continue
        tile = needed_tile(need, groups, reader, offset, k)
        per_chunk = TPP // len(chunks)
        if len(chunks) == 1:
            put(k, chunks[0][pl.ds(pl.multiple_of(tile * TILE, TILE), TILE), :])
            continue
        for i, chunk in enumerate(chunks):

            @pl.when(lax.div(tile, per_chunk) == i)
            def _():
                row = pl.multiple_of(lax.rem(tile, per_chunk) * TILE, TILE)
                put(k, chunk[pl.ds(row, TILE), :])


def aggregate_kernel(plan, groups, n_sources, n_dense, n_totals, widths, first, need, *refs):
    sources, refs = refs[:n_sources], refs[n_sources:]
    denses, refs = refs[:n_dense], refs[n_dense:]
    if not first:
        start_totals, refs = refs[:n_totals], refs[n_totals:]
    totals, (streamed, feats, sem) = refs[:n_totals], refs[n_totals:]
    starts = [sum(widths[:t]) for t in range(n_totals)]
    fresh = [first] * n_totals

    for operand, index, resident, offset, pieces in plan:
        if not resident:
            copy = pltpu.make_async_copy(denses[operand].at[index], streamed, sem)
            copy.start()
        for part, chunks, whole in pieces:
            cols = pl.ds(starts[part], widths[part])

            def put(k, value):
                feats[pl.ds(k * TILE, TILE), cols] = value

            gather_feats(need, groups, 0, offset, [sources[i] for i in chunks], whole, put)
        if not resident:
            copy.wait()
        lhs = denses[operand][index] if resident else streamed[...]
        parts = [part for part, chunks, whole in pieces]
        low, high = starts[parts[0]], starts[parts[-1]] + widths[parts[-1]]
        term = jnp.dot(lhs, feats[:, low:high], preferred_element_type=jnp.float32)
        for part in parts:
            piece = term[:, starts[part] - low : starts[part] - low + widths[part]]
            if fresh[part]:
                totals[part][...] = piece
            elif plan_first(plan, part) == (operand, index):
                totals[part][...] = start_totals[part][...] + piece
            else:
                totals[part][...] += piece
            fresh[part] = False
    for part in range(n_totals):
        if not first and plan_first(plan, part) is None:
            totals[part][...] = start_totals[part][...]


def finish_kernel(plan, groups, n_sources, n_dense, blocks, pairs, need, *refs):
    sources, refs = refs[:n_sources], refs[n_sources:]
    denses, refs = refs[:n_dense], refs[n_dense:]
    start_total, refs = refs[0], refs[1:]
    outs, (streamed, feats, total, sem) = refs[: 2 * len(pairs)], refs[2 * len(pairs) :]
    own = lax.axis_index("feat")
    size = ROWS // blocks
    for e, (operand, index, resident, offset, pieces) in enumerate(plan):
        ((part, chunks, whole),) = pieces

        def put(k, value):
            feats[e, pl.ds(k * TILE, TILE), :] = value

        gather_feats(need, groups, 0, offset, [sources[i] for i in chunks], whole, put)
    for i, pair in enumerate(pairs):
        rows = pl.ds(pl.multiple_of((lax.div(own, 2) ^ pair) * 2 * size, 2 * size), 2 * size)
        total[...] = start_total[rows, :]
        for e, (operand, index, resident, offset, pieces) in enumerate(plan):
            if resident:
                lhs = denses[operand][index, rows, :]
            else:
                copy = pltpu.make_async_copy(denses[operand].at[index, rows, :], streamed, sem)
                copy.start()
                copy.wait()
                lhs = streamed[...]
            total[...] += jnp.dot(lhs, feats[e], preferred_element_type=jnp.float32)
        for low in range(2):
            block = pl.ds(pl.multiple_of((lax.rem(own, 2) ^ low) * size, size), size)
            outs[2 * i + low][...] = total[block, :].astype(jnp.bfloat16)


def finish(plan, groups, need, sources, denses, start_total, blocks, pairs):
    width = start_total.shape[1]
    vmem = pl.BlockSpec(memory_space=pltpu.VMEM)
    spaces = [None] * len(denses)
    for operand, index, resident, offset, pieces in plan:
        spaces[operand] = vmem if resident else pl.BlockSpec(memory_space=pl.ANY)
    streams = any(not entry[2] for entry in plan)
    rows = 2 * ROWS // blocks
    return pl.pallas_call(
        functools.partial(finish_kernel, plan, groups, len(sources), len(denses), blocks, pairs),
        out_shape=[jax.ShapeDtypeStruct((ROWS // blocks, width), jnp.bfloat16)] * (2 * len(pairs)),
        in_specs=[pl.BlockSpec(memory_space=pltpu.SMEM)] + [vmem] * len(sources) + spaces + [vmem],
        out_specs=[vmem] * (2 * len(pairs)),
        scratch_shapes=[
            pltpu.VMEM((rows, DEPTH) if streams else (8, TILE), jnp.bfloat16),
            pltpu.VMEM((len(plan), DEPTH, width), jnp.bfloat16),
            pltpu.VMEM((rows, width), jnp.float32),
            pltpu.SemaphoreType.DMA,
        ],
        compiler_params=pltpu.CompilerParams(vmem_limit_bytes=STREAM_LIMIT if streams else RESIDENT_LIMIT),
        cost_estimate=pl.CostEstimate(
            flops=2 * len(plan) * len(pairs) * rows * DEPTH * width,
            bytes_accessed=2 * len(plan) * len(pairs) * rows * DEPTH,
            transcendentals=0,
        ),
        name="finish",
    )(need, *sources, *denses, start_total)


def plan_first(plan, part):
    for operand, index, resident, offset, pieces in plan:
        if any(piece[0] == part for piece in pieces):
            return (operand, index)
    return None


def aggregate(plan, groups, need, sources, denses, totals, widths):
    first = totals is None
    n_totals = len(widths)
    smem = pl.BlockSpec(memory_space=pltpu.SMEM)
    vmem = pl.BlockSpec(memory_space=pltpu.VMEM)
    spaces = [None] * len(denses)
    for operand, index, resident, offset, pieces in plan:
        spaces[operand] = vmem if resident else pl.BlockSpec(memory_space=pl.ANY)
    streams = any(not entry[2] for entry in plan)
    scratch = [
        pltpu.VMEM((ROWS, DEPTH) if streams else (8, TILE), jnp.bfloat16),
        pltpu.VMEM((DEPTH, sum(widths)), jnp.bfloat16),
    ]
    out_shape = [jax.ShapeDtypeStruct((ROWS, w), jnp.float32) for w in widths]
    flops = sum(2 * ROWS * DEPTH * sum(widths[p[0]] for p in entry[4]) for entry in plan)
    return pl.pallas_call(
        functools.partial(
            aggregate_kernel, plan, groups, len(sources), len(denses), n_totals, widths, first
        ),
        out_shape=out_shape,
        in_specs=[smem] + [vmem] * len(sources) + spaces + ([] if first else [vmem] * n_totals),
        out_specs=[vmem] * len(out_shape),
        scratch_shapes=scratch + [pltpu.SemaphoreType.DMA],
        compiler_params=pltpu.CompilerParams(vmem_limit_bytes=STREAM_LIMIT if streams else RESIDENT_LIMIT),
        cost_estimate=pl.CostEstimate(
            flops=flops, bytes_accessed=len(plan) * ROWS * DEPTH * 2, transcendentals=0
        ),
        name="aggregate",
    )(need, *sources, *denses, *([] if first else totals))


def pick_kernel(reader, offset, groups, need, *refs):
    chunks, out = refs[:-1], refs[-1]

    def put(k, value):
        out[pl.ds(k * TILE, TILE), :] = value

    gather_feats(need, groups, reader, offset, chunks, True, put)


def pick(need, chunks, reader, offset, groups):
    vmem = pl.BlockSpec(memory_space=pltpu.VMEM)
    return pl.pallas_call(
        functools.partial(pick_kernel, reader, offset, groups),
        out_shape=jax.ShapeDtypeStruct((DEPTH, chunks[0].shape[1]), chunks[0].dtype),
        in_specs=[pl.BlockSpec(memory_space=pltpu.SMEM)] + [vmem] * len(chunks),
        out_specs=vmem,
        compiler_params=pltpu.CompilerParams(vmem_limit_bytes=4 * MIB),
        name="pick",
    )(need, *chunks)


def product_kernel(terms, starts, shard, first, final, w, *refs):
    parts, refs = refs[:terms], refs[terms:]
    start_total, refs = (None, refs) if first else (refs[0], refs[1:])
    own = lax.axis_index("feat")
    cols = w.shape[1]
    step = 2 * TILE

    def write(j):
        return pltpu.make_async_copy(refs[1].at[j], refs[0].at[:, pl.ds(j * step, step)], refs[2].at[j])

    for j in range(cols // step):
        band = pl.ds(j * step, step)
        total = None if first else start_total[:, band]
        for i in range(0, terms, 2):
            pair = range(i, min(i + 2, terms))
            x = jnp.concatenate([parts[t][...] for t in pair], axis=1)
            rows = []
            for t in pair:
                m, column = starts[t]
                row = pl.multiple_of((own ^ m) * shard + column, TILE)
                rows.append(w[pl.ds(row, parts[t].shape[1]), band])
            term = jnp.dot(x, jnp.concatenate(rows, axis=0), preferred_element_type=jnp.float32)
            total = term if total is None else total + term
        if final:
            refs[1][j] = jnp.maximum(total, 0.0).astype(jnp.bfloat16)
            write(j).start()
        else:
            refs[0][:, band] = total
    if final:
        for j in range(cols // step):
            write(j).wait()


def product(operands, starts, shard, w, start_total, final):
    rows = operands[0].shape[0]
    _, cols = w.shape
    bands = cols // (2 * TILE)
    vmem = pl.BlockSpec(memory_space=pltpu.VMEM)
    first = start_total is None
    scratch = [pltpu.VMEM((bands, rows, 2 * TILE), jnp.bfloat16), pltpu.SemaphoreType.DMA((bands,))]
    return pl.pallas_call(
        functools.partial(product_kernel, len(operands), starts, shard, first, final),
        out_shape=jax.ShapeDtypeStruct((rows, cols), jnp.bfloat16 if final else jnp.float32),
        in_specs=[vmem] * (1 + len(operands) + (0 if first else 1)),
        out_specs=pl.BlockSpec(memory_space=pl.ANY) if final else vmem,
        scratch_shapes=scratch if final else [],
        compiler_params=pltpu.CompilerParams(vmem_limit_bytes=10 * MIB),
        cost_estimate=pl.CostEstimate(
            flops=2 * rows * cols * sum(x.shape[1] for x in operands), bytes_accessed=8 * rows * cols, transcendentals=0
        ),
        name="product",
    )(w, *operands, *([] if first else [start_total]))


def slot_table(groups, tile_row, tile_panel, tile_slot, counts):
    slots = lax.iota(jnp.int32, tile_row.shape[0])
    key = (tile_panel * TPP + tile_row) * NEED + tile_slot
    key = jnp.where(slots < counts[0], key, -1)
    places = lax.iota(jnp.int32, groups * PER_PANEL)
    return jnp.max(jnp.where(key[None, :] == places[:, None], slots[None, :] + 1, 0), axis=1)


def ring_pairs(groups, way):
    order = [2 * p if p < groups // 2 else 2 * (groups - 1 - p) + 1 for p in range(groups)]
    return [(order[p], order[(p + way) % groups]) for p in range(groups)]


def per_device(features, tiles, tile_row, tile_panel, tile_slot, counts, need_list, weight):
    width = features.shape[1]
    groups = lax.axis_size("rows")
    blocks = lax.axis_size("feat")
    far = groups // 2
    cuts = part_count(width)
    part = width // cuts
    widths = (part,) * cuts
    last = cuts - 1
    need = need_list.reshape(-1)

    def send(array, way):
        return lax.ppermute(array, "rows", ring_pairs(groups, way))

    held = {}
    for c in range(cuts):
        column = features[:, c * part : (c + 1) * part]
        for way in (1, -1):
            n = chunk_count(way, c)
            held[way, 0, c] = ([column[i * ROWS // n : (i + 1) * ROWS // n] for i in range(n)], True)
    for d in range(1, far + 1):
        for c in range(cuts):
            for way in (1, -1):
                end = hop_end(way, c, far)
                chunks = held.get((way, d - 1, c), (None,))[0]
                if d < end:
                    held[way, d, c] = ([send(x, way) for x in chunks], True)
                elif d == end:
                    chosen = pick(need, chunks, way, way - way * d, groups)
                    held[way, d, c] = ([send(chosen, way)], False)

    table = slot_table(groups, tile_row, tile_panel, tile_slot, counts)
    stages = [[0]] + [[-d, d] for d in range(1, far)] + [[far]]

    def is_resident(d):
        return sum(len(stage) for stage in stages[d:]) <= RESIDENT_PANELS

    dense = []
    for d in range(far + 1):
        if d in (0, 2) or is_resident(d) != is_resident(d - 1):
            upto = next((e for e in range(d + 1, far + 1) if e == 2 or is_resident(e) != is_resident(d)), far + 1)
            dense += densify(stages[d:upto], is_resident(d), groups, table, tiles)

    def add(totals, entries, columns, pairs=None):
        sources, operands, plan = [], [], []
        for way, d, parts in entries:
            if d not in operands:
                operands.append(d)
            offset = -way * d
            pieces = []
            for c in parts:
                chunks, whole = held[-1 if d == 0 else way, d, c]
                pieces.append((columns.index(c), tuple(range(len(sources), len(sources) + len(chunks))), whole))
                sources += chunks
            index = stages[d].index(offset) if d < far else 0
            plan.append((operands.index(d), index, is_resident(d), offset, tuple(pieces)))
        sizes = tuple(widths[c] for c in columns)
        if pairs is not None:
            arrays = [dense[d] for d in operands]
            return finish(tuple(plan), groups, need, sources, arrays, totals[0], blocks, pairs)
        return aggregate(tuple(plan), groups, need, sources, [dense[d] for d in operands], totals, sizes)

    every = list(range(cuts))
    totals = add(None, [(1, 0, every)], every)
    for d in range(1, far - 2):
        totals = add(totals, [(1, d, every), (-1, d, every)], every)
    d = far - 2
    if cuts > 1:
        early = [(-1, d, every), (1, d, [0]), (1, d + 1, [0])]
        totals = add(totals, early, every)
        rest = add([totals[1]], [(1, d, [1]), (-1, d + 1, [1])], [1])
        ends = [
            (totals[0], [(-1, d + 1, [0]), (1, far, [0])]),
            (rest[0], [(1, d + 1, [1]), (-1, far, [1])]),
        ]
    else:
        totals = add(totals, [(1, d, every), (-1, d, every)], every)
        totals = add(totals, [(1, d + 1, every), (-1, d + 1, every)], every)
        ends = [(totals[0], [(1, far, every)])]

    finished = {}
    for c, (total, entries) in enumerate(ends):
        for pairs in (tuple(range(1, blocks // 2)), (0,)):
            for pair, outs in zip(pairs, halves(add([total], entries, [c], pairs) if pairs else [])):
                finished[c, 2 * pair], finished[c, 2 * pair + 1] = outs

    def exchange(c, m):
        if m == 0:
            return finished[c, 0]
        return lax.ppermute(finished[c, m], "feat", [(f, f ^ m) for f in range(blocks)])

    order = [(c, m) for c in range(cuts) for m in reversed(range(blocks))]
    arrived = {key: exchange(*key) for key in order}
    soon = [(c, 0) for c in range(cuts)] + [(c, m) for c in range(last) for m in range(2, blocks)]
    late = [(c, 1) for c in range(cuts)] + [(last, m) for m in range(2, blocks)]

    def multiply(keys, start_total, final):
        starts = tuple((m, c * part) for c, m in keys)
        return product([arrived[key] for key in keys], starts, width, weight, start_total, final)

    return multiply(late, multiply(soon, None, False), True)


def halves(outs):
    return [(outs[i], outs[i + 1]) for i in range(0, len(outs), 2)]


def part_count(width):
    return 2 if width % (2 * TILE) == 0 else 1


def chunk_count(way, c):
    return 2 if way > 0 and c == 1 else 1


def hop_end(way, c, far):
    return far if (way > 0) == (c == 0) else far - 1


def solution(mesh):
    return jax.shard_map(
        per_device,
        mesh=mesh,
        in_specs=(
            P("rows", "feat"),
            P("rows", None, None),
            P("rows"),
            P("rows"),
            P("rows"),
            P("rows"),
            P(),
            P(),
        ),
        out_specs=P(("rows", "feat"), None),
        check_vma=False,
    )
```

```python
import functools

import jax
import jax.numpy as jnp
from jax import lax
from jax.experimental import pallas as pl
from jax.experimental.pallas import tpu as pltpu
from jax.sharding import PartitionSpec as P


TILE = 128
TPP = 16
NEED = 8
PER_PANEL = TPP * NEED
ROWS = TPP * TILE
DEPTH = NEED * TILE
MIB = 1024 * 1024
RESIDENT_PANELS = 8
RESIDENT_LIMIT = 9 * MIB
STREAM_LIMIT = 14 * MIB
DENSIFY_LIMIT = 38 * MIB


def place_tiles(panel, table, tiles, dense, sem):
    base = panel * PER_PANEL

    def row_step(row, found):
        for k in range(NEED):
            slot = table[base + row * NEED + k]
            rows = pl.ds(pl.multiple_of(row * TILE, TILE), TILE)
            cols = pl.ds(k * TILE, TILE)

            @pl.when(slot > 0)
            def _():
                pltpu.make_async_copy(tiles.at[slot - 1], dense.at[rows, cols], sem).start()

            @pl.when(slot == 0)
            def _():
                dense[rows, cols] = jnp.zeros((TILE, TILE), jnp.bfloat16)

            found = found + jnp.where(slot > 0, 1, 0)
        return found

    return lax.fori_loop(0, TPP, row_step, 0)


def await_tiles(found, tiles, dense, sem):
    def wait_one(i, c):
        pltpu.make_async_copy(tiles.at[0], dense.at[pl.ds(0, TILE), pl.ds(0, TILE)], sem).wait()
        return c

    lax.fori_loop(0, found, wait_one, 0)


def densify_kernel(stages, resident, groups, table, tiles, *refs):
    outs, (dense, tile_sem, out_sem) = refs[: len(stages)], refs[len(stages) :]
    entries = [(out, e, o) for out, stage in zip(outs, stages) for e, o in enumerate(stage)]
    if resident:
        found = [
            place_tiles(group_at(o, groups), table, tiles, out.at[e], tile_sem.at[0]) for out, e, o in entries
        ]
        out, e, o = entries[0]
        await_tiles(sum(found), tiles, out.at[e], tile_sem.at[0])
        return
    buffers = dense.shape[0]

    def store(i):
        out, e, _ = entries[i]
        return pltpu.make_async_copy(dense.at[i % buffers], out.at[e], out_sem.at[i % buffers])

    for i, (out, e, o) in enumerate(entries):
        buf = i % buffers
        if i >= buffers:
            store(i - buffers).wait()
        found = place_tiles(group_at(o, groups), table, tiles, dense.at[buf], tile_sem.at[buf])
        await_tiles(found, tiles, dense.at[buf], tile_sem.at[buf])
        store(i).start()
    for i in range(max(0, len(entries) - buffers), len(entries)):
        store(i).wait()


def densify(stages, resident, groups, table, tiles):
    buffers = 1 if resident else 2
    out_space = pltpu.VMEM if resident else pl.ANY
    entries = sum(len(stage) for stage in stages)
    return pl.pallas_call(
        functools.partial(densify_kernel, stages, resident, groups),
        out_shape=[jax.ShapeDtypeStruct((len(stage), ROWS, DEPTH), jnp.bfloat16) for stage in stages],
        in_specs=[pl.BlockSpec(memory_space=pltpu.SMEM), pl.BlockSpec(memory_space=pl.ANY)],
        out_specs=[pl.BlockSpec(memory_space=out_space)] * len(stages),
        scratch_shapes=[
            pltpu.VMEM((8, TILE) if resident else (buffers, ROWS, DEPTH), jnp.bfloat16),
            pltpu.SemaphoreType.DMA((buffers,)),
            pltpu.SemaphoreType.DMA((buffers,)),
        ],
        compiler_params=pltpu.CompilerParams(vmem_limit_bytes=max(10 * MIB, DENSIFY_LIMIT - 2 * entries * ROWS * DEPTH)),
        cost_estimate=pl.CostEstimate(flops=0, bytes_accessed=2 * entries * ROWS * DEPTH, transcendentals=0),
        name="densify",
    )(table, tiles)


def group_at(offset, groups):
    own = lax.axis_index("rows")
    place = jnp.where(lax.rem(own, 2) == 0, lax.div(own, 2), groups - 1 - lax.div(own, 2))
    place = lax.rem(place + offset + groups, groups)
    return jnp.where(place < groups // 2, 2 * place, 2 * (groups - 1 - place) + 1)


def needed_tile(need, groups, reader, offset, k):
    return need[(group_at(reader, groups) * groups + group_at(offset, groups)) * NEED + k]


def gather_feats(need, groups, reader, offset, chunks, whole, put):
    for k in range(NEED):
        if not whole:
            put(k, chunks[0][pl.ds(k * TILE, TILE), :])
            continue
        tile = needed_tile(need, groups, reader, offset, k)
        per_chunk = TPP // len(chunks)
        if len(chunks) == 1:
            put(k, chunks[0][pl.ds(pl.multiple_of(tile * TILE, TILE), TILE), :])
            continue
        for i, chunk in enumerate(chunks):

            @pl.when(lax.div(tile, per_chunk) == i)
            def _():
                row = pl.multiple_of(lax.rem(tile, per_chunk) * TILE, TILE)
                put(k, chunk[pl.ds(row, TILE), :])


def aggregate_kernel(plan, groups, n_sources, n_dense, n_totals, widths, first, need, *refs):
    sources, refs = refs[:n_sources], refs[n_sources:]
    denses, refs = refs[:n_dense], refs[n_dense:]
    if not first:
        start_totals, refs = refs[:n_totals], refs[n_totals:]
    totals, (streamed, feats, sem) = refs[:n_totals], refs[n_totals:]
    starts = [sum(widths[:t]) for t in range(n_totals)]
    fresh = [first] * n_totals

    for operand, index, resident, offset, pieces in plan:
        if not resident:
            copy = pltpu.make_async_copy(denses[operand].at[index], streamed, sem)
            copy.start()
        for part, chunks, whole in pieces:
            cols = pl.ds(starts[part], widths[part])

            def put(k, value):
                feats[pl.ds(k * TILE, TILE), cols] = value

            gather_feats(need, groups, 0, offset, [sources[i] for i in chunks], whole, put)
        if not resident:
            copy.wait()
        lhs = denses[operand][index] if resident else streamed[...]
        parts = [part for part, chunks, whole in pieces]
        low, high = starts[parts[0]], starts[parts[-1]] + widths[parts[-1]]
        term = jnp.dot(lhs, feats[:, low:high], preferred_element_type=jnp.float32)
        for part in parts:
            piece = term[:, starts[part] - low : starts[part] - low + widths[part]]
            if fresh[part]:
                totals[part][...] = piece
            elif plan_first(plan, part) == (operand, index):
                totals[part][...] = start_totals[part][...] + piece
            else:
                totals[part][...] += piece
            fresh[part] = False
    for part in range(n_totals):
        if not first and plan_first(plan, part) is None:
            totals[part][...] = start_totals[part][...]


def finish_kernel(plan, groups, n_sources, n_dense, blocks, firsts, run, need, *refs):
    sources, refs = refs[:n_sources], refs[n_sources:]
    denses, refs = refs[:n_dense], refs[n_dense:]
    start_total, refs = refs[0], refs[1:]
    outs, (streamed, feats, total, sem) = refs[: run * len(firsts)], refs[run * len(firsts) :]
    own = lax.axis_index("feat")
    size = ROWS // blocks
    for e, (operand, index, resident, offset, pieces) in enumerate(plan):
        ((part, chunks, whole),) = pieces

        def put(k, value):
            feats[e, pl.ds(k * TILE, TILE), :] = value

        gather_feats(need, groups, 0, offset, [sources[i] for i in chunks], whole, put)
    for i, first in enumerate(firsts):
        rows = pl.ds(pl.multiple_of((lax.div(own, run) ^ (first // run)) * run * size, run * size), run * size)
        total[...] = start_total[rows, :]
        for e, (operand, index, resident, offset, pieces) in enumerate(plan):
            if resident:
                lhs = denses[operand][index, rows, :]
            else:
                copy = pltpu.make_async_copy(denses[operand].at[index, rows, :], streamed, sem)
                copy.start()
                copy.wait()
                lhs = streamed[...]
            total[...] += jnp.dot(lhs, feats[e], preferred_element_type=jnp.float32)
        for low in range(run):
            block = pl.ds(pl.multiple_of((lax.rem(own, run) ^ low) * size, size), size)
            outs[run * i + low][...] = total[block, :].astype(jnp.bfloat16)


def finish(plan, groups, need, sources, denses, start_total, blocks, firsts, run):
    width = start_total.shape[1]
    vmem = pl.BlockSpec(memory_space=pltpu.VMEM)
    spaces = [None] * len(denses)
    for operand, index, resident, offset, pieces in plan:
        spaces[operand] = vmem if resident else pl.BlockSpec(memory_space=pl.ANY)
    streams = any(not entry[2] for entry in plan)
    rows = run * ROWS // blocks
    return pl.pallas_call(
        functools.partial(finish_kernel, plan, groups, len(sources), len(denses), blocks, firsts, run),
        out_shape=[jax.ShapeDtypeStruct((ROWS // blocks, width), jnp.bfloat16)] * (run * len(firsts)),
        in_specs=[pl.BlockSpec(memory_space=pltpu.SMEM)] + [vmem] * len(sources) + spaces + [vmem],
        out_specs=[vmem] * (run * len(firsts)),
        scratch_shapes=[
            pltpu.VMEM((rows, DEPTH) if streams else (8, TILE), jnp.bfloat16),
            pltpu.VMEM((len(plan), DEPTH, width), jnp.bfloat16),
            pltpu.VMEM((rows, width), jnp.float32),
            pltpu.SemaphoreType.DMA,
        ],
        compiler_params=pltpu.CompilerParams(vmem_limit_bytes=STREAM_LIMIT if streams else RESIDENT_LIMIT),
        cost_estimate=pl.CostEstimate(
            flops=2 * len(plan) * len(firsts) * rows * DEPTH * width,
            bytes_accessed=2 * len(plan) * len(firsts) * rows * DEPTH,
            transcendentals=0,
        ),
        name="finish",
    )(need, *sources, *denses, start_total)


def plan_first(plan, part):
    for operand, index, resident, offset, pieces in plan:
        if any(piece[0] == part for piece in pieces):
            return (operand, index)
    return None


def aggregate(plan, groups, need, sources, denses, totals, widths):
    first = totals is None
    n_totals = len(widths)
    smem = pl.BlockSpec(memory_space=pltpu.SMEM)
    vmem = pl.BlockSpec(memory_space=pltpu.VMEM)
    spaces = [None] * len(denses)
    for operand, index, resident, offset, pieces in plan:
        spaces[operand] = vmem if resident else pl.BlockSpec(memory_space=pl.ANY)
    streams = any(not entry[2] for entry in plan)
    scratch = [
        pltpu.VMEM((ROWS, DEPTH) if streams else (8, TILE), jnp.bfloat16),
        pltpu.VMEM((DEPTH, sum(widths)), jnp.bfloat16),
    ]
    out_shape = [jax.ShapeDtypeStruct((ROWS, w), jnp.float32) for w in widths]
    flops = sum(2 * ROWS * DEPTH * sum(widths[p[0]] for p in entry[4]) for entry in plan)
    return pl.pallas_call(
        functools.partial(
            aggregate_kernel, plan, groups, len(sources), len(denses), n_totals, widths, first
        ),
        out_shape=out_shape,
        in_specs=[smem] + [vmem] * len(sources) + spaces + ([] if first else [vmem] * n_totals),
        out_specs=[vmem] * len(out_shape),
        scratch_shapes=scratch + [pltpu.SemaphoreType.DMA],
        compiler_params=pltpu.CompilerParams(vmem_limit_bytes=STREAM_LIMIT if streams else RESIDENT_LIMIT),
        cost_estimate=pl.CostEstimate(
            flops=flops, bytes_accessed=len(plan) * ROWS * DEPTH * 2, transcendentals=0
        ),
        name="aggregate",
    )(need, *sources, *denses, *([] if first else totals))


def pick_kernel(reader, offset, groups, need, *refs):
    chunks, out = refs[:-1], refs[-1]

    def put(k, value):
        out[pl.ds(k * TILE, TILE), :] = value

    gather_feats(need, groups, reader, offset, chunks, True, put)


def pick(need, chunks, reader, offset, groups):
    vmem = pl.BlockSpec(memory_space=pltpu.VMEM)
    return pl.pallas_call(
        functools.partial(pick_kernel, reader, offset, groups),
        out_shape=jax.ShapeDtypeStruct((DEPTH, chunks[0].shape[1]), chunks[0].dtype),
        in_specs=[pl.BlockSpec(memory_space=pltpu.SMEM)] + [vmem] * len(chunks),
        out_specs=vmem,
        compiler_params=pltpu.CompilerParams(vmem_limit_bytes=4 * MIB),
        name="pick",
    )(need, *chunks)


def product_kernel(terms, starts, shard, first, final, w, *refs):
    parts, refs = refs[:terms], refs[terms:]
    start_total, refs = (None, refs) if first else (refs[0], refs[1:])
    own = lax.axis_index("feat")
    cols = w.shape[1]
    step = 2 * TILE

    def write(j):
        return pltpu.make_async_copy(refs[1].at[j], refs[0].at[:, pl.ds(j * step, step)], refs[2].at[j])

    for j in range(cols // step):
        band = pl.ds(j * step, step)
        total = None if first else start_total[:, band]
        for i in range(0, terms, 2):
            pair = range(i, min(i + 2, terms))
            x = jnp.concatenate([parts[t][...] for t in pair], axis=1)
            rows = []
            for t in pair:
                m, column = starts[t]
                row = pl.multiple_of((own ^ m) * shard + column, TILE)
                rows.append(w[pl.ds(row, parts[t].shape[1]), band])
            term = jnp.dot(x, jnp.concatenate(rows, axis=0), preferred_element_type=jnp.float32)
            total = term if total is None else total + term
        if final:
            refs[1][j] = jnp.maximum(total, 0.0).astype(jnp.bfloat16)
            write(j).start()
        else:
            refs[0][:, band] = total
    if final:
        for j in range(cols // step):
            write(j).wait()


def product(operands, starts, shard, w, start_total, final):
    rows = operands[0].shape[0]
    _, cols = w.shape
    bands = cols // (2 * TILE)
    vmem = pl.BlockSpec(memory_space=pltpu.VMEM)
    first = start_total is None
    scratch = [pltpu.VMEM((bands, rows, 2 * TILE), jnp.bfloat16), pltpu.SemaphoreType.DMA((bands,))]
    return pl.pallas_call(
        functools.partial(product_kernel, len(operands), starts, shard, first, final),
        out_shape=jax.ShapeDtypeStruct((rows, cols), jnp.bfloat16 if final else jnp.float32),
        in_specs=[vmem] * (1 + len(operands) + (0 if first else 1)),
        out_specs=pl.BlockSpec(memory_space=pl.ANY) if final else vmem,
        scratch_shapes=scratch if final else [],
        compiler_params=pltpu.CompilerParams(vmem_limit_bytes=10 * MIB),
        cost_estimate=pl.CostEstimate(
            flops=2 * rows * cols * sum(x.shape[1] for x in operands), bytes_accessed=8 * rows * cols, transcendentals=0
        ),
        name="product",
    )(w, *operands, *([] if first else [start_total]))


def slot_table(groups, tile_row, tile_panel, tile_slot, counts):
    slots = lax.iota(jnp.int32, tile_row.shape[0])
    key = (tile_panel * TPP + tile_row) * NEED + tile_slot
    key = jnp.where(slots < counts[0], key, -1)
    places = lax.iota(jnp.int32, groups * PER_PANEL)
    return jnp.max(jnp.where(key[None, :] == places[:, None], slots[None, :] + 1, 0), axis=1)


def ring_pairs(groups, way):
    order = [2 * p if p < groups // 2 else 2 * (groups - 1 - p) + 1 for p in range(groups)]
    return [(order[p], order[(p + way) % groups]) for p in range(groups)]


def per_device(features, tiles, tile_row, tile_panel, tile_slot, counts, need_list, weight):
    width = features.shape[1]
    groups = lax.axis_size("rows")
    blocks = lax.axis_size("feat")
    far = groups // 2
    cuts = part_count(width)
    part = width // cuts
    widths = (part,) * cuts
    last = cuts - 1
    need = need_list.reshape(-1)

    def send(array, way):
        return lax.ppermute(array, "rows", ring_pairs(groups, way))

    held = {}
    for c in range(cuts):
        column = features[:, c * part : (c + 1) * part]
        for way in (1, -1):
            n = chunk_count(way, c)
            held[way, 0, c] = ([column[i * ROWS // n : (i + 1) * ROWS // n] for i in range(n)], True)
    for d in range(1, far + 1):
        for c in range(cuts):
            for way in (1, -1):
                end = hop_end(way, c, far)
                chunks = held.get((way, d - 1, c), (None,))[0]
                if d < end:
                    held[way, d, c] = ([send(x, way) for x in chunks], True)
                elif d == end:
                    chosen = pick(need, chunks, way, way - way * d, groups)
                    held[way, d, c] = ([send(chosen, way)], False)

    table = slot_table(groups, tile_row, tile_panel, tile_slot, counts)
    stages = [[0]] + [[-d, d] for d in range(1, far)] + [[far]]

    def is_resident(d):
        return sum(len(stage) for stage in stages[d:]) <= RESIDENT_PANELS

    dense = []
    for d in range(far + 1):
        if d in (0, 2) or is_resident(d) != is_resident(d - 1):
            upto = next((e for e in range(d + 1, far + 1) if e == 2 or is_resident(e) != is_resident(d)), far + 1)
            dense += densify(stages[d:upto], is_resident(d), groups, table, tiles)

    def add(totals, entries, columns, firsts=None, run=1):
        sources, operands, plan = [], [], []
        for way, d, parts in entries:
            if d not in operands:
                operands.append(d)
            offset = -way * d
            pieces = []
            for c in parts:
                chunks, whole = held[-1 if d == 0 else way, d, c]
                pieces.append((columns.index(c), tuple(range(len(sources), len(sources) + len(chunks))), whole))
                sources += chunks
            index = stages[d].index(offset) if d < far else 0
            plan.append((operands.index(d), index, is_resident(d), offset, tuple(pieces)))
        sizes = tuple(widths[c] for c in columns)
        if firsts is not None:
            arrays = [dense[d] for d in operands]
            return finish(tuple(plan), groups, need, sources, arrays, totals[0], blocks, firsts, run)
        return aggregate(tuple(plan), groups, need, sources, [dense[d] for d in operands], totals, sizes)

    every = list(range(cuts))
    totals = add(None, [(1, 0, every)], every)
    for d in range(1, far - 2):
        totals = add(totals, [(1, d, every), (-1, d, every)], every)
    d = far - 2
    if cuts > 1:
        early = [(-1, d, every), (1, d, [0]), (1, d + 1, [0])]
        totals = add(totals, early, every)
        rest = add([totals[1]], [(1, d, [1]), (-1, d + 1, [1])], [1])
        ends = [
            (totals[0], [(-1, d + 1, [0]), (1, far, [0])]),
            (rest[0], [(1, d + 1, [1]), (-1, far, [1])]),
        ]
    else:
        totals = add(totals, [(1, d, every), (-1, d, every)], every)
        totals = add(totals, [(1, d + 1, every), (-1, d + 1, every)], every)
        ends = [(totals[0], [(1, far, every)])]

    finished = {}

    def complete(c, firsts, run):
        if firsts:
            outs = add([ends[c][0]], ends[c][1], [c], firsts, run)
            finished.update({(c, m + low): outs[run * i + low] for i, m in enumerate(firsts) for low in range(run)})

    for c in range(cuts):
        if c < last:
            for m in reversed(range(2, blocks)):
                complete(c, (m,), 1)
        else:
            complete(c, tuple(range(2, blocks, 2)), 2)
        complete(c, (0,), 2)

    def exchange(c, m):
        if m == 0:
            return finished[c, 0]
        return lax.ppermute(finished[c, m], "feat", [(f, f ^ m) for f in range(blocks)])

    order = [(c, m) for c in range(cuts) for m in reversed(range(blocks))]
    arrived = {key: exchange(*key) for key in order}
    soon = [(c, m) for m in range(2) for c in range(cuts)] + [(c, m) for c in range(last) for m in range(2, blocks)]
    late = [(last, m) for m in range(2, blocks)]

    def multiply(keys, start_total, final):
        starts = tuple((m, c * part) for c, m in keys)
        return product([arrived[key] for key in keys], starts, width, weight, start_total, final)

    return multiply(late, multiply(soon, None, False), True)


def part_count(width):
    return 2 if width % (2 * TILE) == 0 else 1


def chunk_count(way, c):
    return 2 if way > 0 and c == 1 else 1


def hop_end(way, c, far):
    return far if (way > 0) == (c == 0) else far - 1


def solution(mesh):
    return jax.shard_map(
        per_device,
        mesh=mesh,
        in_specs=(
            P("rows", "feat"),
            P("rows", None, None),
            P("rows"),
            P("rows"),
            P("rows"),
            P("rows"),
            P(),
            P(),
        ),
        out_specs=P(("rows", "feat"), None),
        check_vma=False,
    )
```

```python
import functools

import jax
import jax.numpy as jnp
from jax import lax
from jax.experimental import pallas as pl
from jax.experimental.pallas import tpu as pltpu
from jax.sharding import PartitionSpec as P


TILE = 128
TPP = 16
NEED = 8
PER_PANEL = TPP * NEED
ROWS = TPP * TILE
DEPTH = NEED * TILE
MIB = 1024 * 1024
RESIDENT_PANELS = 8
RESIDENT_LIMIT = 9 * MIB
STREAM_LIMIT = 14 * MIB
DENSIFY_LIMIT = 38 * MIB


def place_tiles(panel, table, tiles, dense, sem):
    base = panel * PER_PANEL

    def row_step(row, found):
        for k in range(NEED):
            slot = table[base + row * NEED + k]
            rows = pl.ds(pl.multiple_of(row * TILE, TILE), TILE)
            cols = pl.ds(k * TILE, TILE)

            @pl.when(slot > 0)
            def _():
                pltpu.make_async_copy(tiles.at[slot - 1], dense.at[rows, cols], sem).start()

            @pl.when(slot == 0)
            def _():
                dense[rows, cols] = jnp.zeros((TILE, TILE), jnp.bfloat16)

            found = found + jnp.where(slot > 0, 1, 0)
        return found

    return lax.fori_loop(0, TPP, row_step, 0)


def await_tiles(found, tiles, dense, sem):
    def wait_one(i, c):
        pltpu.make_async_copy(tiles.at[0], dense.at[pl.ds(0, TILE), pl.ds(0, TILE)], sem).wait()
        return c

    lax.fori_loop(0, found, wait_one, 0)


def densify_kernel(stages, resident, groups, table, tiles, *refs):
    outs, (dense, tile_sem, out_sem) = refs[: len(stages)], refs[len(stages) :]
    entries = [(out, e, o) for out, stage in zip(outs, stages) for e, o in enumerate(stage)]
    if resident:
        found = [
            place_tiles(group_at(o, groups), table, tiles, out.at[e], tile_sem.at[0]) for out, e, o in entries
        ]
        out, e, o = entries[0]
        await_tiles(sum(found), tiles, out.at[e], tile_sem.at[0])
        return
    buffers = dense.shape[0]

    def store(i):
        out, e, _ = entries[i]
        return pltpu.make_async_copy(dense.at[i % buffers], out.at[e], out_sem.at[i % buffers])

    for i, (out, e, o) in enumerate(entries):
        buf = i % buffers
        if i >= buffers:
            store(i - buffers).wait()
        found = place_tiles(group_at(o, groups), table, tiles, dense.at[buf], tile_sem.at[buf])
        await_tiles(found, tiles, dense.at[buf], tile_sem.at[buf])
        store(i).start()
    for i in range(max(0, len(entries) - buffers), len(entries)):
        store(i).wait()


def densify(stages, resident, groups, table, tiles):
    buffers = 1 if resident else 2
    out_space = pltpu.VMEM if resident else pl.ANY
    entries = sum(len(stage) for stage in stages)
    return pl.pallas_call(
        functools.partial(densify_kernel, stages, resident, groups),
        out_shape=[jax.ShapeDtypeStruct((len(stage), ROWS, DEPTH), jnp.bfloat16) for stage in stages],
        in_specs=[pl.BlockSpec(memory_space=pltpu.SMEM), pl.BlockSpec(memory_space=pl.ANY)],
        out_specs=[pl.BlockSpec(memory_space=out_space)] * len(stages),
        scratch_shapes=[
            pltpu.VMEM((8, TILE) if resident else (buffers, ROWS, DEPTH), jnp.bfloat16),
            pltpu.SemaphoreType.DMA((buffers,)),
            pltpu.SemaphoreType.DMA((buffers,)),
        ],
        compiler_params=pltpu.CompilerParams(vmem_limit_bytes=max(10 * MIB, DENSIFY_LIMIT - 2 * entries * ROWS * DEPTH)),
        cost_estimate=pl.CostEstimate(flops=0, bytes_accessed=2 * entries * ROWS * DEPTH, transcendentals=0),
        name="densify",
    )(table, tiles)


def group_at(offset, groups):
    own = lax.axis_index("rows")
    place = jnp.where(lax.rem(own, 2) == 0, lax.div(own, 2), groups - 1 - lax.div(own, 2))
    place = lax.rem(place + offset + groups, groups)
    return jnp.where(place < groups // 2, 2 * place, 2 * (groups - 1 - place) + 1)


def needed_tile(need, groups, reader, offset, k):
    return need[(group_at(reader, groups) * groups + group_at(offset, groups)) * NEED + k]


def gather_feats(need, groups, reader, offset, chunks, whole, put):
    for k in range(NEED):
        if not whole:
            put(k, chunks[0][pl.ds(k * TILE, TILE), :])
            continue
        tile = needed_tile(need, groups, reader, offset, k)
        per_chunk = TPP // len(chunks)
        if len(chunks) == 1:
            put(k, chunks[0][pl.ds(pl.multiple_of(tile * TILE, TILE), TILE), :])
            continue
        for i, chunk in enumerate(chunks):

            @pl.when(lax.div(tile, per_chunk) == i)
            def _():
                row = pl.multiple_of(lax.rem(tile, per_chunk) * TILE, TILE)
                put(k, chunk[pl.ds(row, TILE), :])


def aggregate_kernel(plan, groups, n_sources, n_dense, n_totals, widths, first, need, *refs):
    sources, refs = refs[:n_sources], refs[n_sources:]
    denses, refs = refs[:n_dense], refs[n_dense:]
    if not first:
        start_totals, refs = refs[:n_totals], refs[n_totals:]
    totals, (streamed, feats, sem) = refs[:n_totals], refs[n_totals:]
    starts = [sum(widths[:t]) for t in range(n_totals)]
    fresh = [first] * n_totals

    for operand, index, resident, offset, pieces in plan:
        if not resident:
            copy = pltpu.make_async_copy(denses[operand].at[index], streamed, sem)
            copy.start()
        for part, chunks, whole in pieces:
            cols = pl.ds(starts[part], widths[part])

            def put(k, value):
                feats[pl.ds(k * TILE, TILE), cols] = value

            gather_feats(need, groups, 0, offset, [sources[i] for i in chunks], whole, put)
        if not resident:
            copy.wait()
        lhs = denses[operand][index] if resident else streamed[...]
        parts = [part for part, chunks, whole in pieces]
        low, high = starts[parts[0]], starts[parts[-1]] + widths[parts[-1]]
        term = jnp.dot(lhs, feats[:, low:high], preferred_element_type=jnp.float32)
        for part in parts:
            piece = term[:, starts[part] - low : starts[part] - low + widths[part]]
            if fresh[part]:
                totals[part][...] = piece
            elif plan_first(plan, part) == (operand, index):
                totals[part][...] = start_totals[part][...] + piece
            else:
                totals[part][...] += piece
            fresh[part] = False
    for part in range(n_totals):
        if not first and plan_first(plan, part) is None:
            totals[part][...] = start_totals[part][...]


def finish_kernel(jobs, n_sources, n_dense, blocks, partners, *refs):
    sources, refs = refs[:n_sources], refs[n_sources:]
    denses, refs = refs[:n_dense], refs[n_dense:]
    totals, refs = refs[: len(jobs)], refs[len(jobs) :]
    outs, (streamed, sem) = refs[: len(jobs) * len(partners)], refs[len(jobs) * len(partners) :]
    own = lax.axis_index("feat")
    size = ROWS // blocks
    for c, plan in enumerate(jobs):
        for i, m in enumerate(partners):
            rows = pl.ds(pl.multiple_of((own ^ m) * size, size), size)
            total = totals[c][rows, :]
            for operand, index, resident, source in plan:
                if resident:
                    lhs = denses[operand][index, rows, :]
                else:
                    copy = pltpu.make_async_copy(denses[operand].at[index, rows, :], streamed, sem)
                    copy.start()
                    copy.wait()
                    lhs = streamed[...]
                total = total + jnp.dot(lhs, sources[source][...], preferred_element_type=jnp.float32)
            outs[c * len(partners) + i][...] = total.astype(jnp.bfloat16)


def finish(jobs, sources, denses, totals, blocks, partners):
    vmem = pl.BlockSpec(memory_space=pltpu.VMEM)
    entries = [entry for plan in jobs for entry in plan]
    spaces = [None] * len(denses)
    for operand, index, resident, source in entries:
        spaces[operand] = vmem if resident else pl.BlockSpec(memory_space=pl.ANY)
    streams = any(not entry[2] for entry in entries)
    rows = ROWS // blocks
    width = totals[0].shape[1]
    work = len(entries) * len(partners) * rows * DEPTH
    return pl.pallas_call(
        functools.partial(finish_kernel, jobs, len(sources), len(denses), blocks, partners),
        out_shape=[jax.ShapeDtypeStruct((rows, width), jnp.bfloat16)] * (len(jobs) * len(partners)),
        in_specs=[vmem] * len(sources) + spaces + [vmem] * len(totals),
        out_specs=[vmem] * (len(jobs) * len(partners)),
        scratch_shapes=[
            pltpu.VMEM((rows, DEPTH) if streams else (8, TILE), jnp.bfloat16),
            pltpu.SemaphoreType.DMA,
        ],
        compiler_params=pltpu.CompilerParams(vmem_limit_bytes=RESIDENT_LIMIT),
        cost_estimate=pl.CostEstimate(flops=2 * work * width, bytes_accessed=2 * work, transcendentals=0),
        name="finish",
    )(*sources, *denses, *totals)


def plan_first(plan, part):
    for operand, index, resident, offset, pieces in plan:
        if any(piece[0] == part for piece in pieces):
            return (operand, index)
    return None


def aggregate(plan, groups, need, sources, denses, totals, widths):
    first = totals is None
    n_totals = len(widths)
    smem = pl.BlockSpec(memory_space=pltpu.SMEM)
    vmem = pl.BlockSpec(memory_space=pltpu.VMEM)
    spaces = [None] * len(denses)
    for operand, index, resident, offset, pieces in plan:
        spaces[operand] = vmem if resident else pl.BlockSpec(memory_space=pl.ANY)
    streams = any(not entry[2] for entry in plan)
    scratch = [
        pltpu.VMEM((ROWS, DEPTH) if streams else (8, TILE), jnp.bfloat16),
        pltpu.VMEM((DEPTH, sum(widths)), jnp.bfloat16),
    ]
    out_shape = [jax.ShapeDtypeStruct((ROWS, w), jnp.float32) for w in widths]
    flops = sum(2 * ROWS * DEPTH * sum(widths[p[0]] for p in entry[4]) for entry in plan)
    return pl.pallas_call(
        functools.partial(
            aggregate_kernel, plan, groups, len(sources), len(denses), n_totals, widths, first
        ),
        out_shape=out_shape,
        in_specs=[smem] + [vmem] * len(sources) + spaces + ([] if first else [vmem] * n_totals),
        out_specs=[vmem] * len(out_shape),
        scratch_shapes=scratch + [pltpu.SemaphoreType.DMA],
        compiler_params=pltpu.CompilerParams(vmem_limit_bytes=STREAM_LIMIT if streams else RESIDENT_LIMIT),
        cost_estimate=pl.CostEstimate(
            flops=flops, bytes_accessed=len(plan) * ROWS * DEPTH * 2, transcendentals=0
        ),
        name="aggregate",
    )(need, *sources, *denses, *([] if first else totals))


def pick_kernel(reader, offset, groups, need, *refs):
    chunks, out = refs[:-1], refs[-1]

    def put(k, value):
        out[pl.ds(k * TILE, TILE), :] = value

    gather_feats(need, groups, reader, offset, chunks, True, put)


def pick(need, chunks, reader, offset, groups):
    vmem = pl.BlockSpec(memory_space=pltpu.VMEM)
    return pl.pallas_call(
        functools.partial(pick_kernel, reader, offset, groups),
        out_shape=jax.ShapeDtypeStruct((DEPTH, chunks[0].shape[1]), chunks[0].dtype),
        in_specs=[pl.BlockSpec(memory_space=pltpu.SMEM)] + [vmem] * len(chunks),
        out_specs=vmem,
        compiler_params=pltpu.CompilerParams(vmem_limit_bytes=4 * MIB),
        name="pick",
    )(need, *chunks)


def product_kernel(terms, starts, shard, first, final, w, *refs):
    parts, refs = refs[:terms], refs[terms:]
    start_total, refs = (None, refs) if first else (refs[0], refs[1:])
    own = lax.axis_index("feat")
    cols = w.shape[1]
    step = 2 * TILE

    def write(j):
        return pltpu.make_async_copy(refs[1].at[j], refs[0].at[:, pl.ds(j * step, step)], refs[2].at[j])

    for j in range(cols // step):
        band = pl.ds(j * step, step)
        total = None if first else start_total[:, band]
        for i in range(0, terms, 2):
            pair = range(i, min(i + 2, terms))
            x = jnp.concatenate([parts[t][...] for t in pair], axis=1)
            rows = []
            for t in pair:
                m, column = starts[t]
                row = pl.multiple_of((own ^ m) * shard + column, TILE)
                rows.append(w[pl.ds(row, parts[t].shape[1]), band])
            term = jnp.dot(x, jnp.concatenate(rows, axis=0), preferred_element_type=jnp.float32)
            total = term if total is None else total + term
        if final:
            refs[1][j] = jnp.maximum(total, 0.0).astype(jnp.bfloat16)
            write(j).start()
        else:
            refs[0][:, band] = total
    if final:
        for j in range(cols // step):
            write(j).wait()


def product(operands, starts, shard, w, start_total, final):
    rows = operands[0].shape[0]
    _, cols = w.shape
    bands = cols // (2 * TILE)
    vmem = pl.BlockSpec(memory_space=pltpu.VMEM)
    first = start_total is None
    scratch = [pltpu.VMEM((bands, rows, 2 * TILE), jnp.bfloat16), pltpu.SemaphoreType.DMA((bands,))]
    return pl.pallas_call(
        functools.partial(product_kernel, len(operands), starts, shard, first, final),
        out_shape=jax.ShapeDtypeStruct((rows, cols), jnp.bfloat16 if final else jnp.float32),
        in_specs=[vmem] * (1 + len(operands) + (0 if first else 1)),
        out_specs=pl.BlockSpec(memory_space=pl.ANY) if final else vmem,
        scratch_shapes=scratch if final else [],
        compiler_params=pltpu.CompilerParams(vmem_limit_bytes=10 * MIB),
        cost_estimate=pl.CostEstimate(
            flops=2 * rows * cols * sum(x.shape[1] for x in operands), bytes_accessed=8 * rows * cols, transcendentals=0
        ),
        name="product",
    )(w, *operands, *([] if first else [start_total]))


def slot_table(groups, tile_row, tile_panel, tile_slot, counts):
    slots = lax.iota(jnp.int32, tile_row.shape[0])
    key = (tile_panel * TPP + tile_row) * NEED + tile_slot
    key = jnp.where(slots < counts[0], key, -1)
    places = lax.iota(jnp.int32, groups * PER_PANEL)
    return jnp.max(jnp.where(key[None, :] == places[:, None], slots[None, :] + 1, 0), axis=1)


def ring_pairs(groups, way):
    order = [2 * p if p < groups // 2 else 2 * (groups - 1 - p) + 1 for p in range(groups)]
    return [(order[p], order[(p + way) % groups]) for p in range(groups)]


def per_device(features, tiles, tile_row, tile_panel, tile_slot, counts, need_list, weight):
    width = features.shape[1]
    groups = lax.axis_size("rows")
    blocks = lax.axis_size("feat")
    far = groups // 2
    cuts = part_count(width)
    part = width // cuts
    widths = (part,) * cuts
    last = cuts - 1
    need = need_list.reshape(-1)

    def send(array, way):
        return lax.ppermute(array, "rows", ring_pairs(groups, way))

    held = {}
    for c in range(cuts):
        column = features[:, c * part : (c + 1) * part]
        for way in (1, -1):
            n = chunk_count(way, c)
            held[way, 0, c] = ([column[i * ROWS // n : (i + 1) * ROWS // n] for i in range(n)], True)
    for d in range(1, far + 1):
        for c in range(cuts):
            for way in (1, -1):
                end = hop_end(way, c, far)
                chunks = held.get((way, d - 1, c), (None,))[0]
                if d < end:
                    held[way, d, c] = ([send(x, way) for x in chunks], True)
                elif d == end:
                    chosen = pick(need, chunks, way, way - way * d, groups)
                    held[way, d, c] = ([send(chosen, way)], False)

    table = slot_table(groups, tile_row, tile_panel, tile_slot, counts)
    stages = [[0]] + [[-d, d] for d in range(1, far)] + [[far]]

    def is_resident(d):
        return sum(len(stage) for stage in stages[d:]) <= RESIDENT_PANELS

    dense = []
    for d in range(far + 1):
        if d in (0, 2) or is_resident(d) != is_resident(d - 1):
            upto = next((e for e in range(d + 1, far + 1) if e == 2 or is_resident(e) != is_resident(d)), far + 1)
            dense += densify(stages[d:upto], is_resident(d), groups, table, tiles)

    def add(totals, entries, columns):
        sources, operands, plan = [], [], []
        for way, d, parts in entries:
            if d not in operands:
                operands.append(d)
            offset = -way * d
            pieces = []
            for c in parts:
                chunks, whole = held[-1 if d == 0 else way, d, c]
                pieces.append((columns.index(c), tuple(range(len(sources), len(sources) + len(chunks))), whole))
                sources += chunks
            index = stages[d].index(offset) if d < far else 0
            plan.append((operands.index(d), index, is_resident(d), offset, tuple(pieces)))
        sizes = tuple(widths[c] for c in columns)
        return aggregate(tuple(plan), groups, need, sources, [dense[d] for d in operands], totals, sizes)

    every = list(range(cuts))
    totals = add(None, [(1, 0, every)], every)
    for d in range(1, far - 2):
        totals = add(totals, [(1, d, every), (-1, d, every)], every)
    d = far - 2
    if cuts > 1:
        early = [(-1, d, every), (1, d, [0]), (1, d + 1, [0])]
        totals = add(totals, early, every)
        rest = add([totals[1]], [(1, d, [1]), (-1, d + 1, [1])], [1])
        ends = [
            (totals[0], [(-1, d + 1, [0]), (1, far, [0])]),
            (rest[0], [(1, d + 1, [1]), (-1, far, [1])]),
        ]
    else:
        totals = add(totals, [(1, d, every), (-1, d, every)], every)
        totals = add(totals, [(1, d + 1, every), (-1, d + 1, every)], every)
        ends = [(totals[0], [(1, far, every)])]

    finished = {}

    def complete(columns, partners):
        sources, operands, jobs = [], [], []
        for c in columns:
            plan = []
            for way, d, parts in ends[c][1]:
                if d not in operands:
                    operands.append(d)
                index = stages[d].index(-way * d) if d < far else 0
                plan.append((operands.index(d), index, is_resident(d), len(sources)))
                sources += held[way, d, c][0]
            jobs.append(tuple(plan))
        totals = [ends[c][0] for c in columns]
        outs = finish(tuple(jobs), sources, [dense[d] for d in operands], totals, blocks, partners)
        finished.update({(c, m): outs[i * len(partners) + j] for i, c in enumerate(columns) for j, m in enumerate(partners)})

    for c in range(cuts):
        for m in reversed(range(2, blocks)):
            complete([c], (m,))
    complete(every, (0, 1))

    def exchange(c, m):
        if m == 0:
            return finished[c, 0]
        return lax.ppermute(finished[c, m], "feat", [(f, f ^ m) for f in range(blocks)])

    order = [(c, m) for c in range(cuts) for m in reversed(range(blocks))]
    arrived = {key: exchange(*key) for key in order}
    soon = [(c, m) for m in range(2) for c in range(cuts)] + [(c, m) for c in range(last) for m in range(2, blocks)]
    late = [(last, m) for m in range(2, blocks)]

    def multiply(keys, start_total, final):
        starts = tuple((m, c * part) for c, m in keys)
        return product([arrived[key] for key in keys], starts, width, weight, start_total, final)

    return multiply(late, multiply(soon, None, False), True)


def part_count(width):
    return 2 if width % (2 * TILE) == 0 else 1


def chunk_count(way, c):
    return 2 if way > 0 and c == 1 else 1


def hop_end(way, c, far):
    return far if (way > 0) == (c == 0) else far - 1


def solution(mesh):
    return jax.shard_map(
        per_device,
        mesh=mesh,
        in_specs=(
            P("rows", "feat"),
            P("rows", None, None),
            P("rows"),
            P("rows"),
            P("rows"),
            P("rows"),
            P(),
            P(),
        ),
        out_specs=P(("rows", "feat"), None),
        check_vma=False,
    )
```

```python
import functools

import jax
import jax.numpy as jnp
from jax import lax
from jax.experimental import pallas as pl
from jax.experimental.pallas import tpu as pltpu
from jax.sharding import PartitionSpec as P


TILE = 128
TPP = 16
NEED = 8
PER_PANEL = TPP * NEED
ROWS = TPP * TILE
DEPTH = NEED * TILE
MIB = 1024 * 1024
RESIDENT_PANELS = 8
ROW_BLOCK = 512
RESIDENT_LIMIT = 9 * MIB
STREAM_LIMIT = 14 * MIB
DENSIFY_LIMIT = 38 * MIB


def place_tiles(panel, table, tiles, dense, sem):
    base = panel * PER_PANEL

    def row_step(row, found):
        for k in range(NEED):
            slot = table[base + row * NEED + k]
            rows = pl.ds(pl.multiple_of(row * TILE, TILE), TILE)
            cols = pl.ds(k * TILE, TILE)

            @pl.when(slot > 0)
            def _():
                pltpu.make_async_copy(tiles.at[slot - 1], dense.at[rows, cols], sem).start()

            @pl.when(slot == 0)
            def _():
                dense[rows, cols] = jnp.zeros((TILE, TILE), jnp.bfloat16)

            found = found + jnp.where(slot > 0, 1, 0)
        return found

    return lax.fori_loop(0, TPP, row_step, 0)


def await_tiles(found, tiles, dense, sem):
    def wait_one(i, c):
        pltpu.make_async_copy(tiles.at[0], dense.at[pl.ds(0, TILE), pl.ds(0, TILE)], sem).wait()
        return c

    lax.fori_loop(0, found, wait_one, 0)


def densify_kernel(stages, resident, groups, table, tiles, *refs):
    outs, (dense, tile_sem, out_sem) = refs[: len(stages)], refs[len(stages) :]
    entries = [(out, e, o) for out, stage in zip(outs, stages) for e, o in enumerate(stage)]
    if resident:
        found = [
            place_tiles(group_at(o, groups), table, tiles, out.at[e], tile_sem.at[0]) for out, e, o in entries
        ]
        out, e, o = entries[0]
        await_tiles(sum(found), tiles, out.at[e], tile_sem.at[0])
        return
    buffers = dense.shape[0]

    def store(i):
        out, e, _ = entries[i]
        return pltpu.make_async_copy(dense.at[i % buffers], out.at[e], out_sem.at[i % buffers])

    for i, (out, e, o) in enumerate(entries):
        buf = i % buffers
        if i >= buffers:
            store(i - buffers).wait()
        found = place_tiles(group_at(o, groups), table, tiles, dense.at[buf], tile_sem.at[buf])
        await_tiles(found, tiles, dense.at[buf], tile_sem.at[buf])
        store(i).start()
    for i in range(max(0, len(entries) - buffers), len(entries)):
        store(i).wait()


def densify(stages, resident, groups, table, tiles):
    buffers = 1 if resident else 2
    out_space = pltpu.VMEM if resident else pl.ANY
    entries = sum(len(stage) for stage in stages)
    return pl.pallas_call(
        functools.partial(densify_kernel, stages, resident, groups),
        out_shape=[jax.ShapeDtypeStruct((len(stage), ROWS, DEPTH), jnp.bfloat16) for stage in stages],
        in_specs=[pl.BlockSpec(memory_space=pltpu.SMEM), pl.BlockSpec(memory_space=pl.ANY)],
        out_specs=[pl.BlockSpec(memory_space=out_space)] * len(stages),
        scratch_shapes=[
            pltpu.VMEM((8, TILE) if resident else (buffers, ROWS, DEPTH), jnp.bfloat16),
            pltpu.SemaphoreType.DMA((buffers,)),
            pltpu.SemaphoreType.DMA((buffers,)),
        ],
        compiler_params=pltpu.CompilerParams(vmem_limit_bytes=max(10 * MIB, DENSIFY_LIMIT - 2 * entries * ROWS * DEPTH)),
        cost_estimate=pl.CostEstimate(flops=0, bytes_accessed=2 * entries * ROWS * DEPTH, transcendentals=0),
        name="densify",
    )(table, tiles)


def group_at(offset, groups):
    own = lax.axis_index("rows")
    place = jnp.where(lax.rem(own, 2) == 0, lax.div(own, 2), groups - 1 - lax.div(own, 2))
    place = lax.rem(place + offset + groups, groups)
    return jnp.where(place < groups // 2, 2 * place, 2 * (groups - 1 - place) + 1)


def needed_tile(need, groups, reader, offset, k):
    return need[(group_at(reader, groups) * groups + group_at(offset, groups)) * NEED + k]


def gather_feats(need, groups, reader, offset, chunks, whole, put):
    for k in range(NEED):
        if not whole:
            put(k, chunks[0][pl.ds(k * TILE, TILE), :])
            continue
        tile = needed_tile(need, groups, reader, offset, k)
        per_chunk = TPP // len(chunks)
        if len(chunks) == 1:
            put(k, chunks[0][pl.ds(pl.multiple_of(tile * TILE, TILE), TILE), :])
            continue
        for i, chunk in enumerate(chunks):

            @pl.when(lax.div(tile, per_chunk) == i)
            def _():
                row = pl.multiple_of(lax.rem(tile, per_chunk) * TILE, TILE)
                put(k, chunk[pl.ds(row, TILE), :])


def aggregate_kernel(plan, groups, n_sources, n_dense, n_totals, widths, first, need, *refs):
    sources, refs = refs[:n_sources], refs[n_sources:]
    denses, refs = refs[:n_dense], refs[n_dense:]
    if not first:
        start_totals, refs = refs[:n_totals], refs[n_totals:]
    totals, (streamed, feats, sem) = refs[:n_totals], refs[n_totals:]
    if in_row_blocks(plan, n_totals, first):
        for e, (operand, index, resident, offset, pieces) in enumerate(plan):
            ((part, chunks, whole),) = pieces

            def put_entry(k, value):
                feats[e, pl.ds(k * TILE, TILE), :] = value

            gather_feats(need, groups, 0, offset, [sources[i] for i in chunks], whole, put_entry)
        for row in range(0, ROWS, ROW_BLOCK):
            rows = pl.ds(row, ROW_BLOCK)
            total = start_totals[0][rows, :]
            for e, (operand, index, resident, offset, pieces) in enumerate(plan):
                lhs = denses[operand][index, rows, :]
                total = total + jnp.dot(lhs, feats[e], preferred_element_type=jnp.float32)
            totals[0][rows, :] = total
        return
    starts = [sum(widths[:t]) for t in range(n_totals)]
    fresh = [first] * n_totals

    for operand, index, resident, offset, pieces in plan:
        if not resident:
            copy = pltpu.make_async_copy(denses[operand].at[index], streamed, sem)
            copy.start()
        for part, chunks, whole in pieces:
            cols = pl.ds(starts[part], widths[part])

            def put(k, value):
                feats[pl.ds(k * TILE, TILE), cols] = value

            gather_feats(need, groups, 0, offset, [sources[i] for i in chunks], whole, put)
        if not resident:
            copy.wait()
        lhs = denses[operand][index] if resident else streamed[...]
        parts = [part for part, chunks, whole in pieces]
        low, high = starts[parts[0]], starts[parts[-1]] + widths[parts[-1]]
        term = jnp.dot(lhs, feats[:, low:high], preferred_element_type=jnp.float32)
        for part in parts:
            piece = term[:, starts[part] - low : starts[part] - low + widths[part]]
            if fresh[part]:
                totals[part][...] = piece
            elif plan_first(plan, part) == (operand, index):
                totals[part][...] = start_totals[part][...] + piece
            else:
                totals[part][...] += piece
            fresh[part] = False
    for part in range(n_totals):
        if not first and plan_first(plan, part) is None:
            totals[part][...] = start_totals[part][...]


def finish_kernel(jobs, n_sources, n_dense, blocks, partners, *refs):
    sources, refs = refs[:n_sources], refs[n_sources:]
    denses, refs = refs[:n_dense], refs[n_dense:]
    totals, refs = refs[: len(jobs)], refs[len(jobs) :]
    outs, (streamed, sem) = refs[: len(jobs) * len(partners)], refs[len(jobs) * len(partners) :]
    own = lax.axis_index("feat")
    size = ROWS // blocks
    for c, plan in enumerate(jobs):
        for i, m in enumerate(partners):
            rows = pl.ds(pl.multiple_of((own ^ m) * size, size), size)
            total = totals[c][rows, :]
            for operand, index, resident, source in plan:
                if resident:
                    lhs = denses[operand][index, rows, :]
                else:
                    copy = pltpu.make_async_copy(denses[operand].at[index, rows, :], streamed, sem)
                    copy.start()
                    copy.wait()
                    lhs = streamed[...]
                total = total + jnp.dot(lhs, sources[source][...], preferred_element_type=jnp.float32)
            outs[c * len(partners) + i][...] = total.astype(jnp.bfloat16)


def finish(jobs, sources, denses, totals, blocks, partners):
    vmem = pl.BlockSpec(memory_space=pltpu.VMEM)
    entries = [entry for plan in jobs for entry in plan]
    spaces = [None] * len(denses)
    for operand, index, resident, source in entries:
        spaces[operand] = vmem if resident else pl.BlockSpec(memory_space=pl.ANY)
    streams = any(not entry[2] for entry in entries)
    rows = ROWS // blocks
    width = totals[0].shape[1]
    work = len(entries) * len(partners) * rows * DEPTH
    return pl.pallas_call(
        functools.partial(finish_kernel, jobs, len(sources), len(denses), blocks, partners),
        out_shape=[jax.ShapeDtypeStruct((rows, width), jnp.bfloat16)] * (len(jobs) * len(partners)),
        in_specs=[vmem] * len(sources) + spaces + [vmem] * len(totals),
        out_specs=[vmem] * (len(jobs) * len(partners)),
        scratch_shapes=[
            pltpu.VMEM((rows, DEPTH) if streams else (8, TILE), jnp.bfloat16),
            pltpu.SemaphoreType.DMA,
        ],
        compiler_params=pltpu.CompilerParams(vmem_limit_bytes=RESIDENT_LIMIT),
        cost_estimate=pl.CostEstimate(flops=2 * work * width, bytes_accessed=2 * work, transcendentals=0),
        name="finish",
    )(*sources, *denses, *totals)


def plan_first(plan, part):
    for operand, index, resident, offset, pieces in plan:
        if any(piece[0] == part for piece in pieces):
            return (operand, index)
    return None


def in_row_blocks(plan, n_totals, first):
    return n_totals == 1 and not first and all(entry[2] for entry in plan)


def aggregate(plan, groups, need, sources, denses, totals, widths):
    first = totals is None
    n_totals = len(widths)
    by_entry = (len(plan),) if in_row_blocks(plan, n_totals, first) else ()
    smem = pl.BlockSpec(memory_space=pltpu.SMEM)
    vmem = pl.BlockSpec(memory_space=pltpu.VMEM)
    spaces = [None] * len(denses)
    for operand, index, resident, offset, pieces in plan:
        spaces[operand] = vmem if resident else pl.BlockSpec(memory_space=pl.ANY)
    streams = any(not entry[2] for entry in plan)
    scratch = [
        pltpu.VMEM((ROWS, DEPTH) if streams else (8, TILE), jnp.bfloat16),
        pltpu.VMEM(by_entry + (DEPTH, sum(widths)), jnp.bfloat16),
    ]
    out_shape = [jax.ShapeDtypeStruct((ROWS, w), jnp.float32) for w in widths]
    flops = sum(2 * ROWS * DEPTH * sum(widths[p[0]] for p in entry[4]) for entry in plan)
    return pl.pallas_call(
        functools.partial(
            aggregate_kernel, plan, groups, len(sources), len(denses), n_totals, widths, first
        ),
        out_shape=out_shape,
        in_specs=[smem] + [vmem] * len(sources) + spaces + ([] if first else [vmem] * n_totals),
        out_specs=[vmem] * len(out_shape),
        scratch_shapes=scratch + [pltpu.SemaphoreType.DMA],
        compiler_params=pltpu.CompilerParams(vmem_limit_bytes=STREAM_LIMIT if streams else RESIDENT_LIMIT),
        cost_estimate=pl.CostEstimate(
            flops=flops, bytes_accessed=len(plan) * ROWS * DEPTH * 2, transcendentals=0
        ),
        name="aggregate",
    )(need, *sources, *denses, *([] if first else totals))


def pick_kernel(reader, offset, groups, need, *refs):
    chunks, out = refs[:-1], refs[-1]

    def put(k, value):
        out[pl.ds(k * TILE, TILE), :] = value

    gather_feats(need, groups, reader, offset, chunks, True, put)


def pick(need, chunks, reader, offset, groups):
    vmem = pl.BlockSpec(memory_space=pltpu.VMEM)
    return pl.pallas_call(
        functools.partial(pick_kernel, reader, offset, groups),
        out_shape=jax.ShapeDtypeStruct((DEPTH, chunks[0].shape[1]), chunks[0].dtype),
        in_specs=[pl.BlockSpec(memory_space=pltpu.SMEM)] + [vmem] * len(chunks),
        out_specs=vmem,
        compiler_params=pltpu.CompilerParams(vmem_limit_bytes=4 * MIB),
        name="pick",
    )(need, *chunks)


def product_kernel(terms, starts, shard, first, final, w, *refs):
    parts, refs = refs[:terms], refs[terms:]
    start_total, refs = (None, refs) if first else (refs[0], refs[1:])
    own = lax.axis_index("feat")
    cols = w.shape[1]
    step = 2 * TILE

    def write(j):
        return pltpu.make_async_copy(refs[1].at[j], refs[0].at[:, pl.ds(j * step, step)], refs[2].at[j])

    for j in range(cols // step):
        band = pl.ds(j * step, step)
        total = None if first else start_total[:, band]
        for i in range(0, terms, 2):
            pair = range(i, min(i + 2, terms))
            x = jnp.concatenate([parts[t][...] for t in pair], axis=1)
            rows = []
            for t in pair:
                m, column = starts[t]
                row = pl.multiple_of((own ^ m) * shard + column, TILE)
                rows.append(w[pl.ds(row, parts[t].shape[1]), band])
            term = jnp.dot(x, jnp.concatenate(rows, axis=0), preferred_element_type=jnp.float32)
            total = term if total is None else total + term
        if final:
            refs[1][j] = jnp.maximum(total, 0.0).astype(jnp.bfloat16)
            write(j).start()
        else:
            refs[0][:, band] = total
    if final:
        for j in range(cols // step):
            write(j).wait()


def product(operands, starts, shard, w, start_total, final):
    rows = operands[0].shape[0]
    _, cols = w.shape
    bands = cols // (2 * TILE)
    vmem = pl.BlockSpec(memory_space=pltpu.VMEM)
    first = start_total is None
    scratch = [pltpu.VMEM((bands, rows, 2 * TILE), jnp.bfloat16), pltpu.SemaphoreType.DMA((bands,))]
    return pl.pallas_call(
        functools.partial(product_kernel, len(operands), starts, shard, first, final),
        out_shape=jax.ShapeDtypeStruct((rows, cols), jnp.bfloat16 if final else jnp.float32),
        in_specs=[vmem] * (1 + len(operands) + (0 if first else 1)),
        out_specs=pl.BlockSpec(memory_space=pl.ANY) if final else vmem,
        scratch_shapes=scratch if final else [],
        compiler_params=pltpu.CompilerParams(vmem_limit_bytes=10 * MIB),
        cost_estimate=pl.CostEstimate(
            flops=2 * rows * cols * sum(x.shape[1] for x in operands), bytes_accessed=8 * rows * cols, transcendentals=0
        ),
        name="product",
    )(w, *operands, *([] if first else [start_total]))


def slot_table(groups, tile_row, tile_panel, tile_slot, counts):
    slots = lax.iota(jnp.int32, tile_row.shape[0])
    key = (tile_panel * TPP + tile_row) * NEED + tile_slot
    key = jnp.where(slots < counts[0], key, -1)
    places = lax.iota(jnp.int32, groups * PER_PANEL)
    return jnp.max(jnp.where(key[None, :] == places[:, None], slots[None, :] + 1, 0), axis=1)


def ring_pairs(groups, way):
    order = [2 * p if p < groups // 2 else 2 * (groups - 1 - p) + 1 for p in range(groups)]
    return [(order[p], order[(p + way) % groups]) for p in range(groups)]


def per_device(features, tiles, tile_row, tile_panel, tile_slot, counts, need_list, weight):
    width = features.shape[1]
    groups = lax.axis_size("rows")
    blocks = lax.axis_size("feat")
    far = groups // 2
    cuts = part_count(width)
    part = width // cuts
    widths = (part,) * cuts
    last = cuts - 1
    need = need_list.reshape(-1)

    def send(array, way):
        return lax.ppermute(array, "rows", ring_pairs(groups, way))

    held = {}
    for c in range(cuts):
        column = features[:, c * part : (c + 1) * part]
        for way in (1, -1):
            n = chunk_count(way, c)
            held[way, 0, c] = ([column[i * ROWS // n : (i + 1) * ROWS // n] for i in range(n)], True)
    for d in range(1, far + 1):
        for c in range(cuts):
            for way in (1, -1):
                end = hop_end(way, c, far)
                chunks = held.get((way, d - 1, c), (None,))[0]
                if d < end:
                    held[way, d, c] = ([send(x, way) for x in chunks], True)
                elif d == end:
                    chosen = pick(need, chunks, way, way - way * d, groups)
                    held[way, d, c] = ([send(chosen, way)], False)

    table = slot_table(groups, tile_row, tile_panel, tile_slot, counts)
    stages = [[0]] + [[-d, d] for d in range(1, far)] + [[far]]

    def is_resident(d):
        return sum(len(stage) for stage in stages[d:]) <= RESIDENT_PANELS

    dense = []
    for d in range(far + 1):
        if d in (0, 2) or is_resident(d) != is_resident(d - 1):
            upto = next((e for e in range(d + 1, far + 1) if e == 2 or is_resident(e) != is_resident(d)), far + 1)
            dense += densify(stages[d:upto], is_resident(d), groups, table, tiles)

    def add(totals, entries, columns):
        sources, operands, plan = [], [], []
        for way, d, parts in entries:
            if d not in operands:
                operands.append(d)
            offset = -way * d
            pieces = []
            for c in parts:
                chunks, whole = held[-1 if d == 0 else way, d, c]
                pieces.append((columns.index(c), tuple(range(len(sources), len(sources) + len(chunks))), whole))
                sources += chunks
            index = stages[d].index(offset) if d < far else 0
            plan.append((operands.index(d), index, is_resident(d), offset, tuple(pieces)))
        sizes = tuple(widths[c] for c in columns)
        return aggregate(tuple(plan), groups, need, sources, [dense[d] for d in operands], totals, sizes)

    every = list(range(cuts))
    totals = add(None, [(1, 0, every)], every)
    for d in range(1, far - 2):
        totals = add(totals, [(1, d, every), (-1, d, every)], every)
    d = far - 2
    if cuts > 1:
        early = [(-1, d, every), (1, d, [0]), (1, d + 1, [0])]
        totals = add(totals, early, every)
        rest = add([totals[1]], [(1, d, [1]), (-1, d + 1, [1])], [1])
        ends = [
            (totals[0], [(-1, d + 1, [0]), (1, far, [0])]),
            (rest[0], [(1, d + 1, [1]), (-1, far, [1])]),
        ]
    else:
        totals = add(totals, [(1, d, every), (-1, d, every)], every)
        totals = add(totals, [(1, d + 1, every), (-1, d + 1, every)], every)
        ends = [(totals[0], [(1, far, every)])]

    finished = {}

    def complete(columns, partners):
        sources, operands, jobs = [], [], []
        for c in columns:
            plan = []
            for way, d, parts in ends[c][1]:
                if d not in operands:
                    operands.append(d)
                index = stages[d].index(-way * d) if d < far else 0
                plan.append((operands.index(d), index, is_resident(d), len(sources)))
                sources += held[way, d, c][0]
            jobs.append(tuple(plan))
        totals = [ends[c][0] for c in columns]
        outs = finish(tuple(jobs), sources, [dense[d] for d in operands], totals, blocks, partners)
        finished.update({(c, m): outs[i * len(partners) + j] for i, c in enumerate(columns) for j, m in enumerate(partners)})

    for c in range(cuts):
        for m in reversed(range(2, blocks)):
            complete([c], (m,))
    complete(every, (0, 1))

    def exchange(c, m):
        if m == 0:
            return finished[c, 0]
        return lax.ppermute(finished[c, m], "feat", [(f, f ^ m) for f in range(blocks)])

    order = [(c, m) for c in range(cuts) for m in reversed(range(blocks))]
    arrived = {key: exchange(*key) for key in order}
    soon = [(c, m) for m in range(2) for c in range(cuts)] + [(c, m) for c in range(last) for m in range(2, blocks)]
    soon += [(last, m) for m in reversed(range(3, blocks))]
    late = [(last, 2)]

    def multiply(keys, start_total, final):
        starts = tuple((m, c * part) for c, m in keys)
        return product([arrived[key] for key in keys], starts, width, weight, start_total, final)

    return multiply(late, multiply(soon, None, False), True)


def part_count(width):
    return 2 if width % (2 * TILE) == 0 else 1


def chunk_count(way, c):
    return 2 if way > 0 and c == 1 else 1


def hop_end(way, c, far):
    return far if (way > 0) == (c == 0) else far - 1


def solution(mesh):
    return jax.shard_map(
        per_device,
        mesh=mesh,
        in_specs=(
            P("rows", "feat"),
            P("rows", None, None),
            P("rows"),
            P("rows"),
            P("rows"),
            P("rows"),
            P(),
            P(),
        ),
        out_specs=P(("rows", "feat"), None),
        check_vma=False,
    )
```
